128 devices in a mesh: seq: 32 (over z, x, y_lo), tp: 4 (over y_hi, core).
Axes of the slice: x: 4, y: 4 (y_hi: 2, y_lo: 2; y = y_hi * 2 + y_lo), z: 4, core: 2. Of those that a mesh axis runs over, the one named last changes fastest.
Arguments:
- hidden_in: bfloat16 [8192, 1024], P('seq'), may hold values from -6 to 6
- query_weight: bfloat16 [1024, 1024], P(None, 'tp'), may hold values from -0.375 to 0.375
- query_bias: float32 [1024], P('tp'), may hold values from -3.5 to 3.5
- keyval_weight: bfloat16 [2, 1024, 1024], P(None, None, 'tp'), may hold values from -0.1875 to 0.1875
- keyval_bias: float32 [2, 1024], P(None, 'tp'), may hold values from -3 to 3
- out_weight: bfloat16 [1024, 1024], P('tp'), may hold values from -0.75 to 0.75
- out_bias: float32 [1024], replicated, may hold values from -1.75 to 1.75
- up_weight: bfloat16 [1024, 4096], P(None, 'tp'), may hold values from -0.1875 to 0.1875
- up_bias: float32 [4096], P('tp'), may hold values from -3 to 3
- down_weight: bfloat16 [4096, 1024], P('tp'), may hold values from -0.09375 to 0.09375
- down_bias: float32 [1024], replicated, may hold values from -1.75 to 1.75
- norm_gain: float32 [2, 1024], replicated, may hold values from 0.5 to 1.5
- norm_bias: float32 [2, 1024], replicated, may hold values from -1.75 to 1.75
- prefix_keys: bfloat16 [32768, 1024], P('seq', 'tp')
- prefix_values: bfloat16 [32768, 1024], P('seq', 'tp'), may hold values from -6 to 6
- suffix_lengths: int32 [48], replicated, may hold values from 1 to 1024, 8192 in all
- request_group: int32 [48], replicated, may hold values from 0 to 3
- owner_group: int32 [32], replicated, may hold values from 0 to 3, as said below
Outputs:
- layer_out: bfloat16 [8192, 1024], P('seq')
The draws below stay inside these ranges and needn't reach their ends.
Inputs may be any that keep to these rules, and one draw needn't show every extreme that they name: `suffix_lengths`: requests are packed in order and their lengths sum to 8192. `owner_group`: each group is named by exactly 8 entries.
All inputs are finite; a program needn't handle non-finite values.
Results may differ from the reference program's by a relative error of at most 0.013.
The reference program's roundings to bfloat16 on the way count: a program that leaves them out, or rounds other values in their place, can miss the bound.
Values may be sent and summed in bfloat16 or wider, within the bound.
No kernel may reach another device: no remote copies, remote signals or barrier semaphores. Data moves between devices by JAX's collectives and lax.ppermute only.
A program may use at most 128 MiB of HBM per device.

```python
import math
import jax
import jax.numpy as jnp
import numpy as np
from jax import lax

D = 1024
HEADS = 16
HEAD_DIM = 64
FF = 4096
GROUPS = 4
SUF_MAX = 1024
PFX_DEV = 1024
SHARDS = 32
REQS = 48
TOKENS = 8192
PREFIX_ALL = 32768


def draw_prefix_keys(key, part):
    first = jax.random.fold_in(key, 0)
    base = jax.random.normal(first, (PREFIX_ALL, D), jnp.float32)
    return (1.25 * base).astype(jnp.bfloat16)


def draw_owner_group(key, part):
    order = jax.random.permutation(key, SHARDS)
    return (order % GROUPS).astype(jnp.int32)


def set_ends(entries, stream_key, smallest, largest):
    longest = entries.shape.index(max(entries.shape))
    spots = []
    for shift in (0, 1):
        where = [jax.random.randint(jax.random.fold_in(stream_key, axis), (), 0, length) for axis, length in enumerate(entries.shape)]
        where[longest] = (where[longest] + shift) % entries.shape[longest]
        spots.append(tuple(where))
    return entries.at[spots[0]].set(smallest).at[spots[1]].set(largest)


def block_levels(rng, dims, cuts, low, high):
    def one(dim, blocks):
        steps = jax.random.uniform(jax.random.fold_in(jax.random.fold_in(rng, 6), dim), (blocks,), jnp.float32, low / len(cuts), high / len(cuts))
        return jnp.repeat(jnp.exp(steps), dims[dim] // blocks).reshape((-1,) + (1,) * (len(dims) - dim - 1))

    factor_of = one(*cuts[0])
    for cut in cuts[1:]:
        factor_of = factor_of * one(*cut)
    return factor_of


def length_profile(count, total, limit, skew):
    loads = [(1 << 20) // math.isqrt(standing ** skew) + 1 for standing in range(2, count + 1)]
    surplus, given = total - limit - (count - 1), [1] * (count - 1)
    while surplus > 0:
        candidates = [i for i in range(count - 1) if given[i] < limit]
        mass, remaining = sum([loads[i] for i in candidates]), surplus
        for i in candidates:
            extra = min(limit - given[i], max(1, remaining * loads[i] // mass), surplus)
            given[i] = given[i] + extra
            surplus = surplus - extra
    return np.array([limit] + given)


def uneven(key, number_of, total, reach, slope):
    if number_of == 2:
        one = jax.random.randint(key, (), max(1, total - reach), min(reach, total - 1) + 1)
        return jnp.stack([one, total - one])
    sizes = jnp.asarray(length_profile(number_of, total, reach, slope), jnp.int32)
    pairs = (number_of - 1) // 2
    source_of, sink = sizes[1:1 + 2 * pairs:2], sizes[2:2 + 2 * pairs:2]
    room = jnp.minimum(source_of - 1, reach - sink)
    passed = jax.random.randint(jax.random.fold_in(key, 1), (pairs,), 0, 1 << 20) % (room + 1)
    sizes = sizes.at[1:1 + 2 * pairs:2].set(source_of - passed).at[2:2 + 2 * pairs:2].set(sink + passed)
    return sizes[jax.random.permutation(jax.random.fold_in(key, 2), number_of)]


def gaussian(rng, dims, scale, reach, cuts=(), held_as=jnp.bfloat16):
    result = jax.random.normal(rng, dims, jnp.float32) * scale
    if len(cuts) > 0:
        result = block_levels(rng, dims, cuts, -0.22, 0.18) * result
    return jnp.clip(result, min=-reach, max=reach).astype(held_as)


def setup_inputs(seed: int = 0) -> dict:
    streams_of = jax.random.split(jax.random.key(seed), 19)
    return {
        "hidden_in": gaussian(streams_of[0], (TOKENS, D), 1.0, 6.0, ((0, 32),)),
        "query_weight": gaussian(streams_of[1], (D, D), (D // 4) ** -0.5, 0.375, ((1, 4),)),
        "query_bias": gaussian(streams_of[2], (D,), 0.6, 3.5, ((0, 4),), jnp.float32),
        "keyval_weight": gaussian(streams_of[3], (2, D, D), D ** -0.5, 0.1875, ((2, 4),)),
        "keyval_bias": gaussian(streams_of[4], (2, D), 0.5, 3.0, ((1, 4),), jnp.float32),
        "out_weight": gaussian(streams_of[5], (D, D), (D // 16) ** -0.5, 0.75, ((0, 4),)),
        "out_bias": gaussian(streams_of[6], (D,), 0.3, 1.75, (), jnp.float32),
        "up_weight": gaussian(streams_of[7], (D, FF), D ** -0.5, 0.1875, ((1, 4),)),
        "up_bias": gaussian(streams_of[8], (FF,), 0.5, 3.0, ((0, 4),), jnp.float32),
        "down_weight": gaussian(streams_of[9], (FF, D), FF ** -0.5, 0.09375, ((0, 4),)),
        "down_bias": gaussian(streams_of[10], (D,), 0.3, 1.75, (), jnp.float32),
        "norm_gain": jnp.clip(1.0 + 0.1 * jax.random.normal(streams_of[11], (2, D), jnp.float32), 0.5, 1.5),
        "norm_bias": gaussian(streams_of[12], (2, D), 0.3, 1.75, (), jnp.float32),
        "prefix_keys": draw_prefix_keys(jax.random.fold_in(streams_of[18], 71), 0),
        "prefix_values": gaussian(streams_of[14], (PREFIX_ALL, D), 1.0, 6.0, ((0, 32), (1, 4))),
        "suffix_lengths": uneven(streams_of[15], REQS, TOKENS, SUF_MAX, 2).astype(jnp.int32),
        "request_group": set_ends(jax.random.randint(streams_of[16], (REQS,), 0, GROUPS), jax.random.fold_in(streams_of[16], 1), 0, GROUPS - 1).astype(jnp.int32),
        "owner_group": draw_owner_group(jax.random.fold_in(streams_of[18], 71), 0),
    }


neg_big = -1e+30

def layer_norm(values, gain, shift):
    center = values - lax.optimization_barrier(jnp.mean(values, axis=-1, keepdims=True))
    spread = lax.optimization_barrier(jnp.mean(center * center, axis=-1, keepdims=True))
    return center * lax.rsqrt(spread + 1e-05) * gain + shift

def token_groups(index, suffix_lengths, request_group):
    ends = jnp.cumsum(suffix_lengths).astype(jnp.int32)
    request = lax.optimization_barrier(jnp.sum((index[:, None] >= ends[None, :]).astype(jnp.int32), axis=1, dtype=jnp.int32))
    numbers = jnp.arange(suffix_lengths.shape[0], dtype=jnp.int32)
    group = lax.optimization_barrier(jnp.sum(jnp.where(request[:, None] == numbers[None, :], request_group[None, :], 0), axis=1, dtype=jnp.int32))
    return (request, group)

def by_heads(matrix):
    return matrix.reshape(matrix.shape[0], HEADS, HEAD_DIM).transpose(1, 0, 2)

def reference(hidden_in, query_weight, query_bias, keyval_weight, keyval_bias, out_weight, out_bias, up_weight, up_bias, down_weight, down_bias, norm_gain, norm_bias, prefix_keys, prefix_values, suffix_lengths, request_group, owner_group):
    queries = (jnp.dot(hidden_in, query_weight, preferred_element_type=jnp.float32) + query_bias).astype(jnp.bfloat16)
    keys = (jnp.dot(hidden_in, keyval_weight[0], preferred_element_type=jnp.float32) + keyval_bias[0]).astype(jnp.bfloat16)
    values = (jnp.dot(hidden_in, keyval_weight[1], preferred_element_type=jnp.float32) + keyval_bias[1]).astype(jnp.bfloat16)
    token_index = jnp.arange(TOKENS, dtype=jnp.int32)
    request, group = token_groups(token_index, suffix_lengths, request_group)
    prefix_group = owner_group[jnp.arange(PREFIX_ALL, dtype=jnp.int32) // PFX_DEV]
    block = min(512, TOKENS)
    blocks = TOKENS // block

    def one_head(operands):
        head_q, head_k, head_v, head_pk, head_pv = operands

        def one_block(number):
            start = (number * block).astype(jnp.int32)
            rows_q = lax.dynamic_slice_in_dim(head_q, start, block, 0)
            rows_req = lax.dynamic_slice_in_dim(request, start, block, 0)
            rows_grp = lax.dynamic_slice_in_dim(group, start, block, 0)
            rows_idx = start + jnp.arange(block, dtype=jnp.int32)
            allow_pre = rows_grp[:, None] == prefix_group[None, :]
            allow_suf = (rows_req[:, None] == request[None, :]) & (token_index[None, :] <= rows_idx[:, None])
            score_pre = jnp.dot(rows_q, head_pk.T, preferred_element_type=jnp.float32) * 0.125
            score_suf = jnp.dot(rows_q, head_k.T, preferred_element_type=jnp.float32) * 0.125
            score_pre = jnp.where(allow_pre, score_pre, neg_big)
            score_suf = jnp.where(allow_suf, score_suf, neg_big)
            rowmax = jnp.maximum(lax.optimization_barrier(jnp.max(score_pre, axis=1)), lax.optimization_barrier(jnp.max(score_suf, axis=1)))
            weight_pre = jnp.where(allow_pre, jnp.exp(score_pre - rowmax[:, None]), 0.0)
            weight_suf = jnp.where(allow_suf, jnp.exp(score_suf - rowmax[:, None]), 0.0)
            total = lax.optimization_barrier(jnp.sum(weight_pre, axis=1)) + lax.optimization_barrier(jnp.sum(weight_suf, axis=1))
            summed = jnp.dot(weight_pre.astype(jnp.bfloat16), head_pv, preferred_element_type=jnp.float32)
            summed = summed + jnp.dot(weight_suf.astype(jnp.bfloat16), head_v, preferred_element_type=jnp.float32)
            return summed / total[:, None]
        outputs = lax.map(one_block, jnp.arange(blocks, dtype=jnp.int32))
        return outputs.reshape(TOKENS, HEAD_DIM)
    heads_out = lax.map(one_head, (by_heads(queries), by_heads(keys), by_heads(values), by_heads(prefix_keys), by_heads(prefix_values)))
    attended = heads_out.transpose(1, 0, 2).reshape(TOKENS, D).astype(jnp.bfloat16)
    mixed = jnp.dot(attended, out_weight, preferred_element_type=jnp.float32) + out_bias + hidden_in.astype(jnp.float32)
    normed = layer_norm(mixed, norm_gain[0], norm_bias[0]).astype(jnp.bfloat16)
    inner = jax.nn.gelu(jnp.dot(normed, up_weight, preferred_element_type=jnp.float32) + up_bias, approximate=False).astype(jnp.bfloat16)
    final = jnp.dot(inner, down_weight, preferred_element_type=jnp.float32) + down_bias + normed.astype(jnp.float32)
    return layer_norm(final, norm_gain[1], norm_bias[1]).astype(jnp.bfloat16)
```

```python
import functools

import jax
import jax.numpy as jnp
from jax import lax
from jax.experimental import pallas as pl
from jax.experimental.pallas import tpu as pltpu
from jax.sharding import PartitionSpec as P

BF = jnp.bfloat16
F32 = jnp.float32
NEG = -1e30
HD = 64
ROWS = 256
PLANE = 8
DEPTH = 4
TILE = 128
PFX = 1024
TOKENS = 8192
REQS = 48
STATS = 16
VMEM_BYTES = 60 * 1024 * 1024

SEQ_PLANES = [[z * PLANE + a for a in range(PLANE)] for z in range(DEPTH)]


def params(semantics=None):
    return pltpu.CompilerParams(vmem_limit_bytes=VMEM_BYTES, dimension_semantics=semantics)


def whole():
    return pl.BlockSpec(memory_space=pltpu.VMEM)


def anywhere():
    return pl.BlockSpec(memory_space=pl.ANY)


def smem():
    return pl.BlockSpec(memory_space=pltpu.SMEM)


def nt_dot(left, right):
    return lax.dot_general(left, right, (((1,), (1,)), ((), ())), preferred_element_type=F32)


def dot(left, right):
    return jnp.dot(left, right, preferred_element_type=F32)


def project_kernel(x_ref, wq_ref, bq_ref, wkv_ref, bkv_ref, q_ref, kv_ref):
    x = x_ref[...]
    q = (dot(x, wq_ref[...]) + bq_ref[...]).astype(BF) * BF(0.125)
    for n in range(PLANE):
        q_ref[n] = q
    for n in range(2):
        kv_ref[n] = (dot(x, wkv_ref[n]) + bkv_ref[n : n + 1, :]).astype(BF)


def project(x, wq, bq, wkv, bkv):
    cols = wq.shape[1]
    return pl.pallas_call(
        project_kernel,
        out_shape=(
            jax.ShapeDtypeStruct((PLANE, ROWS, cols), BF),
            jax.ShapeDtypeStruct((2, ROWS, cols), BF),
        ),
        in_specs=[whole()] * 5,
        out_specs=(whole(), whole()),
        compiler_params=params(),
        name="project",
    )(x, wq, bq.reshape(1, cols), wkv, bkv)


def attend_kernel(first, last, shifts, *refs):
    shards = len(shifts)
    lengths, groups, owners = refs[:3]
    refs = refs[3:]
    q_hbm = refs[0]
    kv_hbm = refs[1 : 1 + (shards + 1 if first else shards)]
    refs = refs[1 + len(kv_hbm) :]
    if first:
        own_suffix, back_suffix = refs[:2]
        refs = refs[2:]
    else:
        acc_in, state_in = refs[:2]
        refs = refs[2:]
    if last:
        out_ref = refs[0]
        refs = refs[1:]
        acc, state = refs[:2]
        refs = refs[2:]
    else:
        acc, state = refs[:2]
        refs = refs[2:]
    q_s, k_s, v_s, ks_s, vs_s, starts, sem = refs

    place = lax.axis_index("seq")
    depth = place // PLANE
    spot = place % PLANE
    base = depth * (PLANE * ROWS)

    copies = [pltpu.make_async_copy(q_hbm, q_s, sem.at[0])]
    if first:
        copies.append(pltpu.make_async_copy(kv_hbm[0], k_s.at[0], sem.at[1]))
        copies.append(pltpu.make_async_copy(kv_hbm[1], v_s.at[0], sem.at[2]))
        rest = kv_hbm[2:]
        done = 1
        for n, src in enumerate((own_suffix, back_suffix)):
            copies.append(pltpu.make_async_copy(src.at[0], ks_s.at[n], sem.at[3 + 2 * n]))
            copies.append(pltpu.make_async_copy(src.at[1], vs_s.at[n], sem.at[4 + 2 * n]))
    else:
        rest = kv_hbm
        done = 0
        copies.append(pltpu.make_async_copy(acc_in, acc, sem.at[1]))
        copies.append(pltpu.make_async_copy(state_in, state, sem.at[2]))
    for n, src in enumerate(rest):
        copies.append(pltpu.make_async_copy(src.at[0], k_s.at[done + n], sem.at[7 + 2 * n]))
        copies.append(pltpu.make_async_copy(src.at[1], v_s.at[done + n], sem.at[8 + 2 * n]))
    for c in copies:
        c.start()

    def add_start(r, total):
        starts[r] = total
        return total + lengths[r]

    starts[REQS] = lax.fori_loop(0, REQS, add_start, jnp.int32(0))

    lane = lax.broadcasted_iota(jnp.int32, (TILE, 128), 1)
    low = lane < HD
    if first:
        init = jnp.where(lane < 4, F32(NEG), F32(0.0))

        def clear(t, _):
            state[pl.ds(t * TILE, TILE), :] = init
            acc[pl.ds(t * TILE, TILE), :] = jnp.zeros((TILE, 256), F32)
            return 0

        lax.fori_loop(0, PLANE * ROWS // TILE, clear, 0)
    for c in copies:
        c.wait()

    owner_of = [owners[((depth + s) % DEPTH) * PLANE + spot] for s in shifts]

    def step(row, keys, values, ok, mask):
        packed = state[pl.ds(row, TILE), :]
        fresh = packed
        ok2 = jnp.concatenate([ok, ok], axis=0)
        for s in range(2):
            cols = slice(128 * s, 128 * s + 128)
            q = q_s[pl.ds(row, TILE), cols]
            zero = jnp.zeros_like(q)
            both = jnp.concatenate([jnp.where(low, q, zero), jnp.where(low, zero, q)], axis=0)
            scores = nt_dot(both, keys[:, cols])
            if mask is not None:
                mask2 = jnp.concatenate([mask, mask], axis=0)
                scores = jnp.where(mask2, scores, NEG)
            top = jnp.max(scores, axis=1, keepdims=True)
            heads = (2 * s, 2 * s + 1)
            old = jnp.concatenate([packed[:, h : h + 1] for h in heads], axis=0)
            old_total = jnp.concatenate([packed[:, 4 + h : 5 + h] for h in heads], axis=0)
            new = jnp.where(ok2, jnp.maximum(old, top), old)
            weights = jnp.exp(scores - jnp.where(ok2, new, top))
            if mask is not None:
                weights = jnp.where(mask2, weights, 0.0)
            fade = jnp.exp(old - new)
            total = old_total * fade + jnp.where(
                ok2, jnp.sum(weights, axis=1, keepdims=True), 0.0
            )
            part = dot(weights.astype(BF), values[:, cols])
            part = jnp.where(ok2, part, 0.0)
            part = jnp.where(low, part[:TILE], part[TILE:])
            fading = jnp.where(low, fade[:TILE], fade[TILE:])
            acc[pl.ds(row, TILE), cols] = acc[pl.ds(row, TILE), cols] * fading + part
            for n, h in enumerate(heads):
                rows = slice(n * TILE, (n + 1) * TILE)
                fresh = jnp.where(lane == h, new[rows], fresh)
                fresh = jnp.where(lane == 4 + h, total[rows], fresh)
        state[pl.ds(row, TILE), :] = fresh

    def tile_step(t, request):
        row = pl.multiple_of(t * TILE, TILE)
        token0 = base + row
        request = lax.while_loop(lambda r: starts[r + 1] <= token0, lambda r: r + 1, request)
        token = token0 + lax.broadcasted_iota(jnp.int32, (TILE, 1), 0)

        def more(c):
            r = c[0]
            return (r < REQS) & (starts[jnp.minimum(r, REQS)] < token0 + TILE)

        def visit(c):
            r, bits, group, start = c
            here = token >= starts[r]
            g = groups[r]
            return (
                r + 1,
                bits | (jnp.int32(1) << g),
                jnp.where(here, g, group),
                jnp.where(here, starts[r], start),
            )

        zeros = jnp.zeros((TILE, 1), jnp.int32)
        _, bits, group, start = lax.while_loop(more, visit, (request, jnp.int32(0), zeros, zeros))

        def shard(j, _):
            g = owner_of[0]
            for n in range(1, shards):
                g = jnp.where(j == n, owner_of[n], g)

            @pl.when(((bits >> g) & 1) == 1)
            def _():
                step(row, k_s[j], v_s[j], group == g, None)

            return 0

        lax.fori_loop(0, shards, shard, 0)
        if first:

            def suffix(j, _):
                key0 = base - j * (PLANE * ROWS) + spot * ROWS

                @pl.when(
                    (key0 >= 0) & (key0 < token0 + TILE) & (starts[request] < key0 + ROWS)
                )
                def _():
                    key = key0 + lax.broadcasted_iota(jnp.int32, (TILE, ROWS), 1)
                    mask = (key >= start) & (key <= token)
                    ok = (start < key0 + ROWS) & (key0 <= token)
                    step(row, ks_s[j], vs_s[j], ok, mask)

                return 0

            lax.fori_loop(0, 2, suffix, 0)
        return request

    lax.fori_loop(0, PLANE * ROWS // TILE, tile_step, jnp.int32(0))

    if last:

        def finish(b, _):
            for u in range(2):
                row = pl.multiple_of(b * ROWS + u * TILE, TILE)
                packed = state[pl.ds(row, TILE), :]
                lse = jnp.zeros((TILE, 128), F32)
                for s in range(2):
                    scale = []
                    for h in (2 * s, 2 * s + 1):
                        total = packed[:, 4 + h : 5 + h]
                        some = total > 0.0
                        safe = jnp.where(some, total, 1.0)
                        scale.append(jnp.where(some, 1.0 / safe, 0.0))
                        value = jnp.where(some, packed[:, h : h + 1] + jnp.log(safe), NEG)
                        lse = jnp.where(lane == h, value, lse)
                    cols = slice(128 * s, 128 * s + 128)
                    part = acc[pl.ds(row, TILE), cols] * jnp.where(low, scale[0], scale[1])
                    out_ref[b, u * TILE : (u + 1) * TILE, cols] = part.astype(BF)
                rows4 = jnp.transpose(lse)[0:4, :]
                high = rows4.astype(BF).astype(F32)
                mid = (rows4 - high).astype(BF).astype(F32)
                rest4 = rows4 - high - mid
                stats = jnp.concatenate([high, mid, rest4, jnp.zeros_like(high)], axis=0)
                out_ref[b, ROWS : ROWS + STATS, u * TILE : (u + 1) * TILE] = stats.astype(BF)
            return 0

        lax.fori_loop(0, PLANE, finish, 0)


def attend(first, last, shifts, scalars, q, kvs, extra):
    shards = len(shifts)
    tokens = PLANE * ROWS
    acc_shape = (tokens, 256)
    state_shape = (tokens, 128)
    scratch = [
        pltpu.VMEM((tokens, 256), BF),
        pltpu.VMEM((shards, PFX, 256), BF),
        pltpu.VMEM((shards, PFX, 256), BF),
        pltpu.VMEM((2, ROWS, 256), BF),
        pltpu.VMEM((2, ROWS, 256), BF),
        pltpu.SMEM((REQS + 1,), jnp.int32),
        pltpu.SemaphoreType.DMA((7 + 2 * shards,)),
    ]
    if last:
        out_shape = jax.ShapeDtypeStruct((PLANE, ROWS + STATS, 256), BF)
        out_specs = whole()
        scratch = [pltpu.VMEM(acc_shape, F32), pltpu.VMEM(state_shape, F32)] + scratch
    else:
        out_shape = (
            jax.ShapeDtypeStruct(acc_shape, F32),
            jax.ShapeDtypeStruct(state_shape, F32),
        )
        out_specs = (whole(), whole())
    operands = [q.reshape(tokens, 256)] + list(kvs) + list(extra)
    return pl.pallas_call(
        functools.partial(attend_kernel, first, last, shifts),
        out_shape=out_shape,
        in_specs=[smem()] * 3 + [anywhere()] * len(operands),
        out_specs=out_specs,
        scratch_shapes=scratch,
        compiler_params=params(),
        name="attend_first" if first else "attend_rest",
    )(*scalars, *operands)


def merge_kernel(parts_ref, out_ref):
    rows = []
    for i in range(PLANE):
        st = parts_ref[i, ROWS : ROWS + STATS, :].astype(F32)
        rows.append(st[0:4] + st[4:8] + st[8:12])
    top = functools.reduce(jnp.maximum, rows)
    rows = [jnp.exp(r - top) for r in rows]
    total = functools.reduce(jnp.add, rows)
    weights = jnp.concatenate([r / total for r in rows], axis=0)
    weights = jnp.concatenate([weights, jnp.zeros((128 - 4 * PLANE, ROWS), F32)], axis=0)
    tall = jnp.transpose(weights)
    high = tall.astype(BF)
    rest = (tall - high.astype(F32)).astype(BF)
    both = jnp.concatenate([high, rest], axis=1)
    source = lax.broadcasted_iota(jnp.int32, (256, 256), 0) % 128
    column_head = lax.broadcasted_iota(jnp.int32, (256, 256), 1) // HD
    acc = jnp.zeros((ROWS, 256), F32)
    for i in range(PLANE):
        spread = (source == column_head + 4 * i).astype(F32).astype(BF)
        acc = acc + dot(both, spread) * parts_ref[i, 0:ROWS, :].astype(F32)
    out_ref[...] = acc.astype(BF)


def merge(parts):
    return pl.pallas_call(
        merge_kernel,
        out_shape=jax.ShapeDtypeStruct((ROWS, 256), BF),
        in_specs=[whole()],
        out_specs=whole(),
        compiler_params=params(),
        name="merge",
    )(parts)


def normalize(values, gain, shift):
    center = values - jnp.mean(values, axis=-1, keepdims=True)
    spread = jnp.mean(center * center, axis=-1, keepdims=True)
    return center * lax.rsqrt(spread + 1e-05) * gain + shift


def middle_kernel(
    mine, theirs, out_w_mine, out_w_theirs, up_own, up_mate, down_own, down_mate,
    hidden, out_bias, gain, shift, up_bias, normed_ref, part_ref,
    a_s, ow_s, up_s, down_s, sem,
):
    side = lax.axis_index("tp") // 2
    copies = [
        pltpu.make_async_copy(mine, a_s.at[side], sem.at[0]),
        pltpu.make_async_copy(theirs, a_s.at[1 - side], sem.at[1]),
        pltpu.make_async_copy(out_w_mine, ow_s.at[side], sem.at[2]),
        pltpu.make_async_copy(out_w_theirs, ow_s.at[1 - side], sem.at[3]),
        pltpu.make_async_copy(up_own, up_s.at[0], sem.at[4]),
        pltpu.make_async_copy(up_mate, up_s.at[1], sem.at[5]),
        pltpu.make_async_copy(down_own, down_s.at[0], sem.at[6]),
        pltpu.make_async_copy(down_mate, down_s.at[1], sem.at[7]),
    ]
    for c in copies:
        c.start()
    for c in copies[:4]:
        c.wait()
    mixed = out_bias[...] + hidden[...].astype(F32)
    for y in range(2):
        for n in range(2):
            mixed = mixed + dot(a_s[y, n], ow_s[y, n])
    normed = normalize(mixed, gain[0:1, :], shift[0:1, :]).astype(BF)
    normed_ref[...] = normed
    total = None
    for n in range(2):
        copies[4 + n].wait()
        copies[6 + n].wait()
        for c in range(4):
            cols = slice(256 * c, 256 * c + 256)
            up = dot(normed, up_s[n, :, cols]) + up_bias[n : n + 1, cols]
            inner = (0.5 * up * (1.0 + lax.erf(up * F32(0.7071067811865476)))).astype(BF)
            piece = dot(inner, down_s[n, cols, :])
            total = piece if total is None else total + piece
    part_ref[...] = total.astype(BF)


def middle(mine, theirs, weights, hidden, out_bias, gain, shift, up_bias):
    half = hidden.shape[0]
    return pl.pallas_call(
        middle_kernel,
        out_shape=(
            jax.ShapeDtypeStruct((half, 1024), BF),
            jax.ShapeDtypeStruct((half, 1024), BF),
        ),
        in_specs=[anywhere()] * 8 + [whole()] * 5,
        out_specs=(whole(), whole()),
        scratch_shapes=[
            pltpu.VMEM((2, 2, half, 256), BF),
            pltpu.VMEM((2, 2, 256, 1024), BF),
            pltpu.VMEM((2, 1024, 1024), BF),
            pltpu.VMEM((2, 1024, 1024), BF),
            pltpu.SemaphoreType.DMA((8,)),
        ],
        compiler_params=params(),
        name="middle",
    )(mine, theirs, *weights, hidden, out_bias, gain, shift, up_bias)


def final_kernel(own, other, normed, bias, gain, shift, out_ref):
    lowered = own[...].astype(F32) + other[...].astype(F32)
    total = lowered + bias[...] + normed[...].astype(F32)
    out_ref[...] = normalize(total, gain[1:2, :], shift[1:2, :]).astype(BF)


def final(own, other, normed, bias, gain, shift):
    return pl.pallas_call(
        final_kernel,
        out_shape=jax.ShapeDtypeStruct(own.shape, BF),
        in_specs=[whole()] * 6,
        out_specs=whole(),
        compiler_params=params(),
        name="final",
    )(own, other, normed, bias, gain, shift)


def from_depth(value, by):
    pairs = [
        (((z + by) % DEPTH) * PLANE + a, z * PLANE + a) for z in range(DEPTH) for a in range(PLANE)
    ]
    return lax.ppermute(value, "seq", pairs)


def from_tp(value, flip):
    return lax.ppermute(value, "tp", [(i, i ^ flip) for i in range(4)])


def shards(
    hidden_in, query_weight, query_bias, keyval_weight, keyval_bias, out_weight, out_bias,
    up_weight, up_bias, down_weight, down_bias, norm_gain, norm_bias, prefix_keys,
    prefix_values, suffix_lengths, request_group, owner_group,
):
    core = lax.axis_index("tp") % 2
    half = ROWS // 2
    prefix = jnp.stack((prefix_keys, prefix_values))
    ahead = [from_depth(prefix, by) for by in (1, 3, 2)]
    q_copies, own_suffix = project(hidden_in, query_weight, query_bias, keyval_weight, keyval_bias)
    back_suffix = from_depth(own_suffix, 3)
    queries = lax.all_to_all(q_copies, "seq", 0, 0, tiled=True, axis_index_groups=SEQ_PLANES)
    scalars = (suffix_lengths, request_group, owner_group)
    acc, state = attend(
        True,
        False,
        (0, 1, 3),
        scalars,
        queries,
        (prefix_keys, prefix_values, ahead[0], ahead[1]),
        (own_suffix, back_suffix),
    )
    parts = attend(False, True, (2,), scalars, queries, (ahead[2],), (acc, state))
    parts = lax.all_to_all(parts, "seq", 0, 0, tiled=True, axis_index_groups=SEQ_PLANES)
    attended = merge(parts)

    up_mate = from_tp(up_weight, 1)
    down_mate = from_tp(down_weight, 1)
    bias_mate = from_tp(up_bias, 1)
    out_mate = from_tp(out_weight, 1)
    out_mine = jnp.stack((out_weight, out_mate))
    out_theirs = from_tp(out_mine, 2)
    keep = lax.dynamic_slice_in_dim(attended, core * half, half, 0)
    give = lax.dynamic_slice_in_dim(attended, (1 - core) * half, half, 0)
    mine = jnp.stack((keep, from_tp(give, 1)))
    theirs = from_tp(mine, 2)
    hidden_half = lax.dynamic_slice_in_dim(hidden_in, core * half, half, 0)
    normed, part = middle(
        mine,
        theirs,
        (out_mine, out_theirs, up_weight, up_mate, down_weight, down_mate),
        hidden_half,
        out_bias.reshape(1, -1),
        norm_gain,
        norm_bias,
        jnp.stack((up_bias, bias_mate)),
    )
    result = final(part, from_tp(part, 2), normed, down_bias.reshape(1, -1), norm_gain, norm_bias)
    other = from_tp(result, 1)
    first = jnp.where(core == 0, result, other)
    second = jnp.where(core == 0, other, result)
    return jnp.concatenate((first, second), axis=0)


def solution(mesh):
    return jax.shard_map(
        shards,
        mesh=mesh,
        in_specs=(
            P("seq", None),
            P(None, "tp"),
            P("tp"),
            P(None, None, "tp"),
            P(None, "tp"),
            P("tp", None),
            P(),
            P(None, "tp"),
            P("tp"),
            P("tp", None),
            P(),
            P(),
            P(),
            P("seq", "tp"),
            P("seq", "tp"),
            P(),
            P(),
            P(),
        ),
        out_specs=P("seq", None),
        check_vma=False,
    )
```

```python
import functools

import jax
import jax.numpy as jnp
from jax import lax
from jax.experimental import pallas as pl
from jax.experimental.pallas import tpu as pltpu
from jax.sharding import PartitionSpec as P

BF = jnp.bfloat16
F32 = jnp.float32
NEG = -1e30
HD = 64
ROWS = 256
PLANE = 8
DEPTH = 4
TILE = 128
PFX = 1024
TOKENS = 8192
REQS = 48
STATS = 16
VMEM_BYTES = 60 * 1024 * 1024

SEQ_PLANES = [[z * PLANE + a for a in range(PLANE)] for z in range(DEPTH)]


def params(semantics=None):
    return pltpu.CompilerParams(vmem_limit_bytes=VMEM_BYTES, dimension_semantics=semantics)


def whole():
    return pl.BlockSpec(memory_space=pltpu.VMEM)


def anywhere():
    return pl.BlockSpec(memory_space=pl.ANY)


def smem():
    return pl.BlockSpec(memory_space=pltpu.SMEM)


def nt_dot(left, right):
    return lax.dot_general(left, right, (((1,), (1,)), ((), ())), preferred_element_type=F32)


def dot(left, right):
    return jnp.dot(left, right, preferred_element_type=F32)


def project_kernel(x_ref, wq_ref, bq_ref, wkv_ref, bkv_ref, q_ref, kv_ref):
    x = x_ref[...]
    q = (dot(x, wq_ref[...]) + bq_ref[...]).astype(BF) * BF(0.125)
    for n in range(PLANE):
        q_ref[n] = q
    for n in range(2):
        kv_ref[n] = (dot(x, wkv_ref[n]) + bkv_ref[n : n + 1, :]).astype(BF)


def project(x, wq, bq, wkv, bkv):
    cols = wq.shape[1]
    return pl.pallas_call(
        project_kernel,
        out_shape=(
            jax.ShapeDtypeStruct((PLANE, ROWS, cols), BF),
            jax.ShapeDtypeStruct((2, ROWS, cols), BF),
        ),
        in_specs=[whole()] * 5,
        out_specs=(whole(), whole()),
        compiler_params=params(),
        name="project",
    )(x, wq, bq.reshape(1, cols), wkv, bkv)


BOUND = 60.0
WIDE = PLANE * ROWS
TILES = WIDE // TILE


def squares(rows, spread):
    wide = rows.astype(F32)
    return dot((wide * wide).astype(BF), spread)


def attend_kernel(first, shifts, *refs):
    shards = len(shifts)
    lengths, groups, owners = refs[:3]
    refs = refs[3:]
    if first:
        q_hbm, own_k, own_v, kv_up, kv_down = refs[:5]
        kv_hbm = (own_k, own_v, kv_up.at[0], kv_up.at[1], kv_down.at[0], kv_down.at[1])
        refs = refs[5:]
        acc_out, total_out, ref_out, fast_ref = refs[:4]
        refs = refs[4:]
    else:
        fast_in = refs[0]
        q_hbm = refs[1]
        kv_hbm = refs[2 : 2 + 2 * shards]
        refs = refs[2 + 2 * shards :]
        suffixes = refs[:2]
        acc_in, total_in, ref_in = refs[2:5]
        out_ref = refs[5]
        refs = refs[6:]
    acc, total, shift_s, q_s, k_s, v_s, ks_s, vs_s, starts, fast_s, sem = refs

    place = lax.axis_index("seq")
    depth = place // PLANE
    spot = place % PLANE
    base = depth * WIDE

    copies = [pltpu.make_async_copy(q_hbm, q_s, sem.at[0])]
    n_sem = 1
    for n in range(shards):
        copies.append(pltpu.make_async_copy(kv_hbm[2 * n], k_s.at[n], sem.at[n_sem]))
        n_sem += 1
        for s in range(2):
            cols = slice(128 * s, 128 * s + 128)
            copies.append(
                pltpu.make_async_copy(
                    kv_hbm[2 * n + 1].at[:, cols], v_s.at[n, s, :, 0:128], sem.at[n_sem]
                )
            )
            n_sem += 1
    if not first:
        for n in range(2):
            copies.append(pltpu.make_async_copy(suffixes[n].at[0], ks_s.at[n], sem.at[n_sem]))
            n_sem += 1
            for s in range(2):
                cols = slice(128 * s, 128 * s + 128)
                copies.append(
                    pltpu.make_async_copy(
                        suffixes[n].at[1, :, cols], vs_s.at[n, s, :, 0:128], sem.at[n_sem]
                    )
                )
                n_sem += 1
        copies.append(pltpu.make_async_copy(acc_in, acc, sem.at[n_sem]))
        copies.append(pltpu.make_async_copy(total_in, total, sem.at[n_sem + 1]))
        n_sem += 2
    for c in copies:
        c.start()

    def add_start(r, done):
        starts[r] = done
        return done + lengths[r]

    starts[REQS] = lax.fori_loop(0, REQS, add_start, jnp.int32(0))

    for n in range(shards):
        for s in range(2):
            v_s[n, s, :, 128:256] = jnp.ones((PFX, 128), BF)
    if not first:
        for n in range(2):
            for s in range(2):
                vs_s[n, s, :, 128:256] = jnp.ones((ROWS, 128), BF)
    lane = lax.broadcasted_iota(jnp.int32, (TILE, 128), 1)
    low = lane < HD
    row_head = lax.broadcasted_iota(jnp.int32, (256, 128), 0) // HD
    spread = (row_head == lax.broadcasted_iota(jnp.int32, (256, 128), 1)).astype(F32).astype(BF)
    for c in copies:
        c.wait()

    if not first:
        moved = pltpu.make_async_copy(ref_in, shift_s, sem.at[n_sem])
        slow_before = lax.fori_loop(
            0, TILES, lambda t, c: c + (fast_in[t] == 0).astype(jnp.int32), jnp.int32(0)
        )

        @pl.when(slow_before > 0)
        def _():
            moved.start()
            moved.wait()

        @pl.when(slow_before == 0)
        def _():
            shift_s[...] = jnp.zeros((WIDE, 256), F32)

    key_top = jnp.max(squares(k_s[0], spread), axis=0, keepdims=True)
    for n in range(1, shards):
        key_top = jnp.maximum(key_top, jnp.max(squares(k_s[n], spread), axis=0, keepdims=True))
    if not first:
        for n in range(2):
            top = jnp.max(squares(ks_s[n], spread), axis=0, keepdims=True)
            key_top = jnp.maximum(key_top, top)

    def decide(t, slow):
        row = pl.multiple_of(t * TILE, TILE)
        top = jnp.max(squares(q_s[pl.ds(row, TILE), :], spread), axis=0, keepdims=True)
        fast = (jnp.max(top * key_top) < BOUND * BOUND / 1.05).astype(jnp.int32)
        if not first:
            fast = fast * fast_in[t]
        fast_s[t] = fast
        return slow + (1 - fast)

    slow_tiles = lax.fori_loop(0, TILES, decide, jnp.int32(0))

    owner_of = [owners[((depth + s) % DEPTH) * PLANE + spot] for s in shifts]

    def stacked(row, s):
        cols = slice(128 * s, 128 * s + 128)
        q = q_s[pl.ds(row, TILE), cols]
        zero = jnp.zeros_like(q)
        return jnp.concatenate([jnp.where(low, q, zero), jnp.where(low, zero, q)], axis=0)

    def by_head(pair):
        return jnp.where(low, pair[:TILE], pair[TILE:])

    def step_fast(row, keys, values, ok, mask):
        count = keys.shape[0]
        for s in range(2):
            cols = slice(128 * s, 128 * s + 128)
            both = stacked(row, s)
            part = None
            for c in range(count // 256):
                rows = slice(256 * c, 256 * c + 256)
                weights = jnp.exp(nt_dot(both, keys[rows, cols]))
                if mask is not None:
                    weights = jnp.where(jnp.concatenate([mask, mask], axis=0), weights, 0.0)
                piece = dot(weights.astype(BF), values[s, rows, :])
                part = piece if part is None else part + piece
            values_part = jnp.where(ok, by_head(part[:, 0:128]), 0.0)
            total_part = jnp.where(ok, by_head(part[:, 128:256]), 0.0)
            acc[pl.ds(row, TILE), cols] += values_part
            total[pl.ds(row, TILE), cols] += total_part

    def step_slow(row, keys, values, ok, mask):
        for s in range(2):
            cols = slice(128 * s, 128 * s + 128)
            scores = nt_dot(stacked(row, s), keys[:, cols])
            if mask is not None:
                mask2 = jnp.concatenate([mask, mask], axis=0)
                scores = jnp.where(mask2, scores, NEG)
            top = jnp.max(scores, axis=1, keepdims=True)
            before = total[pl.ds(row, TILE), cols]
            old = jnp.where(before > 0.0, shift_s[pl.ds(row, TILE), cols], NEG)
            tops = by_head(jnp.broadcast_to(top, (2 * TILE, 128)))
            new = jnp.where(ok, jnp.maximum(old, tops), old)
            used = jnp.concatenate([new[:, 0:1], new[:, 64:65]], axis=0)
            ok2 = jnp.concatenate([ok, ok], axis=0)
            weights = jnp.exp(scores - jnp.where(ok2, used, top))
            if mask is not None:
                weights = jnp.where(mask2, weights, 0.0)
            part = dot(weights.astype(BF), values[s])
            fade = jnp.exp(old - new)
            acc[pl.ds(row, TILE), cols] = acc[pl.ds(row, TILE), cols] * fade + jnp.where(
                ok, by_head(part[:, 0:128]), 0.0
            )
            total[pl.ds(row, TILE), cols] = before * fade + jnp.where(
                ok, by_head(part[:, 128:256]), 0.0
            )
            shift_s[pl.ds(row, TILE), cols] = jnp.where(ok, new, shift_s[pl.ds(row, TILE), cols])

    def tile_step(t, request):
        row = pl.multiple_of(t * TILE, TILE)
        token0 = base + row
        fast = fast_s[t]
        if first:
            acc[pl.ds(row, TILE), :] = jnp.zeros((TILE, 256), F32)
            total[pl.ds(row, TILE), :] = jnp.zeros((TILE, 256), F32)
            shift_s[pl.ds(row, TILE), :] = jnp.zeros((TILE, 256), F32)
        request = lax.while_loop(lambda r: starts[r + 1] <= token0, lambda r: r + 1, request)
        token = token0 + lax.broadcasted_iota(jnp.int32, (TILE, 1), 0)

        def more(c):
            r = c[0]
            return (r < REQS) & (starts[jnp.minimum(r, REQS)] < token0 + TILE)

        def visit(c):
            r, bits, group, start = c
            here = token >= starts[r]
            g = groups[r]
            return (
                r + 1,
                bits | (jnp.int32(1) << g),
                jnp.where(here, g, group),
                jnp.where(here, starts[r], start),
            )

        zeros = jnp.zeros((TILE, 1), jnp.int32)
        _, bits, group, start = lax.while_loop(more, visit, (request, jnp.int32(0), zeros, zeros))

        def shard(j, _):
            g = owner_of[0]
            for n in range(1, shards):
                g = jnp.where(j == n, owner_of[n], g)
            here = (bits >> g) & 1

            @pl.when((here == 1) & (fast == 1))
            def _():
                step_fast(row, k_s.at[j], v_s.at[j], group == g, None)

            @pl.when((here == 1) & (fast == 0))
            def _():
                step_slow(row, k_s.at[j], v_s.at[j], group == g, None)

            return 0

        lax.fori_loop(0, shards, shard, 0)
        if not first:

            def suffix(j, _):
                key0 = base - j * WIDE + spot * ROWS
                here = (key0 >= 0) & (key0 < token0 + TILE) & (starts[request] < key0 + ROWS)

                def args():
                    key = key0 + lax.broadcasted_iota(jnp.int32, (TILE, ROWS), 1)
                    mask = (key >= start) & (key <= token)
                    ok = (start < key0 + ROWS) & (key0 <= token)
                    return row, ks_s.at[j], vs_s.at[j], ok, mask

                @pl.when(here & (fast == 1))
                def _():
                    step_fast(*args())

                @pl.when(here & (fast == 0))
                def _():
                    step_slow(*args())

                return 0

            lax.fori_loop(0, 2, suffix, 0)
        return request

    lax.fori_loop(0, TILES, tile_step, jnp.int32(0))

    if first:
        outs = [
            pltpu.make_async_copy(acc, acc_out, sem.at[0]),
            pltpu.make_async_copy(total, total_out, sem.at[1]),
        ]
        for c in outs:
            c.start()

        def flag(t, _):
            fast_ref[t] = fast_s[t]
            return 0

        lax.fori_loop(0, TILES, flag, 0)

        @pl.when(slow_tiles > 0)
        def _():
            moved = pltpu.make_async_copy(shift_s, ref_out, sem.at[2])
            moved.start()
            moved.wait()

        for c in outs:
            c.wait()
    else:

        def finish(b, _):
            for u in range(2):
                row = pl.multiple_of(b * ROWS + u * TILE, TILE)
                lse = ()
                for s in range(2):
                    cols = slice(128 * s, 128 * s + 128)
                    summed = total[pl.ds(row, TILE), cols]
                    some = summed > 0.0
                    safe = jnp.where(some, summed, 1.0)
                    part = jnp.where(some, acc[pl.ds(row, TILE), cols] / safe, 0.0)
                    out_ref[b, u * TILE : (u + 1) * TILE, cols] = part.astype(BF)
                    value = jnp.where(
                        some, shift_s[pl.ds(row, TILE), cols] + jnp.log(safe), F32(NEG)
                    )
                    flat = jnp.transpose(value)
                    pair = (flat[0:1, :], flat[64:65, :])
                    lse = lse + pair
                rows4 = jnp.concatenate(lse, axis=0)
                high = rows4.astype(BF).astype(F32)
                mid = (rows4 - high).astype(BF).astype(F32)
                rest4 = rows4 - high - mid
                stats = jnp.concatenate([high, mid, rest4, jnp.zeros_like(high)], axis=0)
                out_ref[b, ROWS : ROWS + STATS, u * TILE : (u + 1) * TILE] = stats.astype(BF)
            return 0

        lax.fori_loop(0, PLANE, finish, 0)


def attend(first, shifts, scalars, flags, q, kvs, extra):
    shards = len(shifts)
    blocks = 1 if first else 2
    state = jax.ShapeDtypeStruct((WIDE, 256), F32)
    scratch = [
        pltpu.VMEM((WIDE, 256), F32),
        pltpu.VMEM((WIDE, 256), F32),
        pltpu.VMEM((WIDE, 256), F32),
        pltpu.VMEM((WIDE, 256), BF),
        pltpu.VMEM((shards, PFX, 256), BF),
        pltpu.VMEM((shards, 2, PFX, 256), BF),
        pltpu.VMEM((blocks, ROWS, 256), BF),
        pltpu.VMEM((blocks, 2, ROWS, 256), BF),
        pltpu.SMEM((REQS + 1,), jnp.int32),
        pltpu.SMEM((TILES,), jnp.int32),
        pltpu.SemaphoreType.DMA((16,)),
    ]
    if first:
        out_shape = (state, state, state, jax.ShapeDtypeStruct((TILES,), jnp.int32))
        out_specs = (anywhere(), anywhere(), anywhere(), smem())
    else:
        out_shape = jax.ShapeDtypeStruct((PLANE, ROWS + STATS, 256), BF)
        out_specs = whole()
    small = list(scalars) + list(flags)
    operands = [q.reshape(WIDE, 256)] + list(kvs) + list(extra)
    return pl.pallas_call(
        functools.partial(attend_kernel, first, shifts),
        out_shape=out_shape,
        in_specs=[smem()] * len(small) + [anywhere()] * len(operands),
        out_specs=out_specs,
        scratch_shapes=scratch,
        compiler_params=params(),
        name="attend_first" if first else "attend_rest",
    )(*small, *operands)


def merge_kernel(parts_ref, weight_ref, keep_ref, give_ref, out_ref):
    rows = []
    for i in range(PLANE):
        st = parts_ref[i, ROWS : ROWS + STATS, :].astype(F32)
        rows.append(st[0:4] + st[4:8] + st[8:12])
    top = functools.reduce(jnp.maximum, rows)
    rows = [jnp.exp(r - top) for r in rows]
    total = functools.reduce(jnp.add, rows)
    weights = jnp.concatenate([r / total for r in rows], axis=0)
    weights = jnp.concatenate([weights, jnp.zeros((128 - 4 * PLANE, ROWS), F32)], axis=0)
    tall = jnp.transpose(weights)
    high = tall.astype(BF)
    rest = (tall - high.astype(F32)).astype(BF)
    both = jnp.concatenate([high, rest], axis=1)
    source = lax.broadcasted_iota(jnp.int32, (256, 256), 0) % 128
    column_head = lax.broadcasted_iota(jnp.int32, (256, 256), 1) // HD
    acc = jnp.zeros((ROWS, 256), F32)
    for i in range(PLANE):
        spread = (source == column_head + 4 * i).astype(F32).astype(BF)
        acc = acc + dot(both, spread) * parts_ref[i, 0:ROWS, :].astype(F32)
    out_ref[...] = acc.astype(BF)
    half = ROWS // 2
    core = lax.axis_index("tp") % 2
    keep_row = pl.multiple_of(core * half, half)
    give_row = pl.multiple_of((1 - core) * half, half)
    give_ref[...] = dot(out_ref[pl.ds(give_row, half), :], weight_ref[...])
    keep_ref[...] = dot(out_ref[pl.ds(keep_row, half), :], weight_ref[...])


def merge(parts, weight):
    half = jax.ShapeDtypeStruct((ROWS // 2, 1024), F32)
    return pl.pallas_call(
        merge_kernel,
        out_shape=(half, half),
        in_specs=[whole()] * 2,
        out_specs=(whole(), whole()),
        scratch_shapes=[pltpu.VMEM((ROWS, 256), BF)],
        compiler_params=params(),
        name="merge",
    )(parts, weight)


def add_kernel(left, right, out_ref):
    out_ref[...] = (left[...] + right[...]).astype(BF)


def add(left, right):
    return pl.pallas_call(
        add_kernel,
        out_shape=jax.ShapeDtypeStruct(left.shape, BF),
        in_specs=[whole()] * 2,
        out_specs=whole(),
        compiler_params=params(),
        name="add",
    )(left, right)


def normalize(values, gain, shift):
    center = values - jnp.mean(values, axis=-1, keepdims=True)
    spread = jnp.mean(center * center, axis=-1, keepdims=True)
    return center * lax.rsqrt(spread + 1e-05) * gain + shift


def middle_kernel(
    up_own, up_mate, down_own, down_mate, mine, theirs, hidden_ref,
    out_bias, gain, shift, bias_own, bias_mate, normed_ref, part_ref, up_s, down_s, sem,
):
    copies = [
        pltpu.make_async_copy(up_own, up_s.at[0], sem.at[0]),
        pltpu.make_async_copy(up_mate, up_s.at[1], sem.at[1]),
        pltpu.make_async_copy(down_own, down_s.at[0], sem.at[2]),
        pltpu.make_async_copy(down_mate, down_s.at[1], sem.at[3]),
    ]
    for c in copies:
        c.start()
    half = ROWS // 2
    row = pl.multiple_of((lax.axis_index("tp") % 2) * half, half)
    hidden = hidden_ref[pl.ds(row, half), :].astype(F32)
    mixed = (mine[...].astype(F32) + theirs[...].astype(F32)) + out_bias[...] + hidden
    normed = normalize(mixed, gain[0:1, :], shift[0:1, :]).astype(BF)
    normed_ref[...] = normed
    total = None
    biases = (bias_own, bias_mate)
    for n in range(2):
        copies[n].wait()
        copies[2 + n].wait()
        for c in range(4):
            cols = slice(256 * c, 256 * c + 256)
            up = dot(normed, up_s[n, :, cols]) + biases[n][:, cols]
            inner = (0.5 * up * (1.0 + lax.erf(up * F32(0.7071067811865476)))).astype(BF)
            piece = dot(inner, down_s[n, cols, :])
            total = piece if total is None else total + piece
    part_ref[...] = total.astype(BF)


def middle(weights, mine, theirs, hidden, out_bias, gain, shift, bias_own, bias_mate):
    half = ROWS // 2
    return pl.pallas_call(
        middle_kernel,
        out_shape=(
            jax.ShapeDtypeStruct((half, 1024), BF),
            jax.ShapeDtypeStruct((half, 1024), BF),
        ),
        in_specs=[anywhere()] * 4 + [whole()] * 8,
        out_specs=(whole(), whole()),
        scratch_shapes=[
            pltpu.VMEM((2, 1024, 1024), BF),
            pltpu.VMEM((2, 1024, 1024), BF),
            pltpu.SemaphoreType.DMA((4,)),
        ],
        compiler_params=params(),
        name="middle",
    )(*weights, mine, theirs, hidden, out_bias, gain, shift, bias_own, bias_mate)


def final_kernel(own, other, normed, bias, gain, shift, out_ref):
    lowered = own[...].astype(F32) + other[...].astype(F32)
    total = lowered + bias[...] + normed[...].astype(F32)
    out_ref[...] = normalize(total, gain[1:2, :], shift[1:2, :]).astype(BF)


def final(own, other, normed, bias, gain, shift):
    return pl.pallas_call(
        final_kernel,
        out_shape=jax.ShapeDtypeStruct(own.shape, BF),
        in_specs=[whole()] * 6,
        out_specs=whole(),
        compiler_params=params(),
        name="final",
    )(own, other, normed, bias, gain, shift)


def from_depth(value, by):
    pairs = [
        (((z + by) % DEPTH) * PLANE + a, z * PLANE + a) for z in range(DEPTH) for a in range(PLANE)
    ]
    return lax.ppermute(value, "seq", pairs)


def from_tp(value, flip):
    return lax.ppermute(value, "tp", [(i, i ^ flip) for i in range(4)])


def shards(
    hidden_in, query_weight, query_bias, keyval_weight, keyval_bias, out_weight, out_bias,
    up_weight, up_bias, down_weight, down_bias, norm_gain, norm_bias, prefix_keys,
    prefix_values, suffix_lengths, request_group, owner_group,
):
    core = lax.axis_index("tp") % 2
    prefix = jnp.stack((prefix_keys, prefix_values))
    kv_up, kv_down = from_depth(prefix, 1), from_depth(prefix, 3)
    k_far, v_far = from_depth(kv_up[0], 1), from_depth(kv_down[1], 3)
    q_copies, own_suffix = project(hidden_in, query_weight, query_bias, keyval_weight, keyval_bias)
    back_suffix = from_depth(own_suffix, 3)
    queries = lax.all_to_all(q_copies, "seq", 0, 0, tiled=True, axis_index_groups=SEQ_PLANES)
    scalars = (suffix_lengths, request_group, owner_group)
    acc, total, shift, fast = attend(
        True,
        (0, 1, 3),
        scalars,
        (),
        queries,
        (prefix_keys, prefix_values, kv_up, kv_down),
        (),
    )
    parts = attend(
        False,
        (2,),
        scalars,
        (fast,),
        queries,
        (k_far, v_far),
        (own_suffix, back_suffix, acc, total, shift),
    )
    parts = lax.all_to_all(parts, "seq", 0, 0, tiled=True, axis_index_groups=SEQ_PLANES)
    up_mate = from_tp(up_weight, 1)
    down_mate = from_tp(down_weight, 1)
    bias_mate = from_tp(up_bias.reshape(1, -1), 1)
    keep, give = merge(parts, out_weight)
    mine = add(keep, from_tp(give, 1))
    normed, part = middle(
        (up_weight, up_mate, down_weight, down_mate),
        mine,
        from_tp(mine, 2),
        hidden_in,
        out_bias.reshape(1, -1),
        norm_gain,
        norm_bias,
        up_bias.reshape(1, -1),
        bias_mate,
    )
    result = final(part, from_tp(part, 2), normed, down_bias.reshape(1, -1), norm_gain, norm_bias)
    other = from_tp(result, 1)
    first = jnp.where(core == 0, result, other)
    second = jnp.where(core == 0, other, result)
    return jnp.concatenate((first, second), axis=0)


def solution(mesh):
    return jax.shard_map(
        shards,
        mesh=mesh,
        in_specs=(
            P("seq", None),
            P(None, "tp"),
            P("tp"),
            P(None, None, "tp"),
            P(None, "tp"),
            P("tp", None),
            P(),
            P(None, "tp"),
            P("tp"),
            P("tp", None),
            P(),
            P(),
            P(),
            P("seq", "tp"),
            P("seq", "tp"),
            P(),
            P(),
            P(),
        ),
        out_specs=P("seq", None),
        check_vma=False,
    )
```

```python
import functools

import jax
import jax.numpy as jnp
from jax import lax
from jax.experimental import pallas as pl
from jax.experimental.pallas import tpu as pltpu
from jax.sharding import PartitionSpec as P

BF = jnp.bfloat16
F32 = jnp.float32
NEG = -1e30
HD = 64
ROWS = 256
PLANE = 8
DEPTH = 4
SUFFIX = 3
TILE = 128
PFX = 1024
TOKENS = 8192
REQS = 48
STATS = 16
VMEM_BYTES = 60 * 1024 * 1024

SEQ_PLANES = [[z * 8 + x * 2 + y for z in range(4) for y in range(2)] for x in range(DEPTH)]


def params(semantics=None):
    return pltpu.CompilerParams(vmem_limit_bytes=VMEM_BYTES, dimension_semantics=semantics)


def whole():
    return pl.BlockSpec(memory_space=pltpu.VMEM)


def anywhere():
    return pl.BlockSpec(memory_space=pl.ANY)


def smem():
    return pl.BlockSpec(memory_space=pltpu.SMEM)


def nt_dot(left, right):
    return lax.dot_general(left, right, (((1,), (1,)), ((), ())), preferred_element_type=F32)


def dot(left, right):
    return jnp.dot(left, right, preferred_element_type=F32)


def project_kernel(x_ref, wq_ref, bq_ref, wkv_ref, bkv_ref, q_ref, kv_ref):
    x = x_ref[...]
    q = (dot(x, wq_ref[...]) + bq_ref[...]).astype(BF) * BF(0.125)
    for n in range(PLANE):
        q_ref[n] = q
    for n in range(2):
        kv_ref[n] = (dot(x, wkv_ref[n]) + bkv_ref[n : n + 1, :]).astype(BF)


def project(x, wq, bq, wkv, bkv):
    cols = wq.shape[1]
    return pl.pallas_call(
        project_kernel,
        out_shape=(
            jax.ShapeDtypeStruct((PLANE, ROWS, cols), BF),
            jax.ShapeDtypeStruct((2, ROWS, cols), BF),
        ),
        in_specs=[whole()] * 5,
        out_specs=(whole(), whole()),
        compiler_params=params(),
        name="project",
    )(x, wq, bq.reshape(1, cols), wkv, bkv)


BOUND = 70.0
WIDE = PLANE * ROWS
TILES = WIDE // TILE


def squares(rows, spread):
    wide = rows.astype(F32)
    return dot((wide * wide).astype(BF), spread)


def attend_kernel(first, shifts, *refs):
    shards = len(shifts)
    lengths, groups, owners = refs[:3]
    refs = refs[3:]
    if first:
        q_hbm = refs[0]
        kv_hbm = refs[1 : 1 + 2 * shards]
        refs = refs[1 + 2 * shards :]
        acc_out, total_out, ref_out, fast_ref = refs[:4]
        refs = refs[4:]
    else:
        fast_in = refs[0]
        q_hbm = refs[1]
        kv_hbm = refs[2 : 2 + 2 * shards]
        refs = refs[2 + 2 * shards :]
        suffixes = refs[:SUFFIX]
        acc_in, total_in, ref_in, out_ref = refs[SUFFIX : SUFFIX + 4]
        refs = refs[SUFFIX + 4 :]
    acc, total, shift_s, q_s, k_s, v_s, ks_s, vs_s, starts, sem = refs

    place = lax.axis_index("seq")
    ring = (place // 2) % DEPTH
    line = place - 2 * ring

    early = [pltpu.make_async_copy(q_hbm, q_s, sem.at[0])]
    late = []
    for n in range(shards):
        early.append(pltpu.make_async_copy(kv_hbm[2 * n], k_s.at[n], sem.at[1 + 2 * n]))
        late.append(pltpu.make_async_copy(kv_hbm[2 * n + 1], v_s.at[n], sem.at[2 + 2 * n]))
    n_sem = 1 + 2 * shards
    if not first:
        for n in range(SUFFIX):
            early.append(pltpu.make_async_copy(suffixes[n].at[0], ks_s.at[n], sem.at[n_sem]))
            late.append(pltpu.make_async_copy(suffixes[n].at[1], vs_s.at[n], sem.at[n_sem + 1]))
            n_sem += 2
        late.append(pltpu.make_async_copy(acc_in, acc, sem.at[n_sem]))
        late.append(pltpu.make_async_copy(total_in, total, sem.at[n_sem + 1]))
        n_sem += 2
    for c in early + late:
        c.start()

    def add_start(r, done):
        starts[r] = done
        return done + lengths[r]

    starts[REQS] = lax.fori_loop(0, REQS, add_start, jnp.int32(0))

    lane = lax.broadcasted_iota(jnp.int32, (TILE, 128), 1)
    low = lane < HD
    wide_head = lax.broadcasted_iota(jnp.int32, (TILE, 256), 1) // HD
    row_head = lax.broadcasted_iota(jnp.int32, (256, 128), 0) // HD
    spread = (row_head == lax.broadcasted_iota(jnp.int32, (256, 128), 1)).astype(F32).astype(BF)
    for c in early:
        c.wait()

    if not first:
        moved = pltpu.make_async_copy(ref_in, shift_s, sem.at[n_sem])
        slow_before = 1 - fast_in[0]

        @pl.when(slow_before > 0)
        def _():
            moved.start()
            moved.wait()

        @pl.when(slow_before == 0)
        def _():
            shift_s[...] = jnp.zeros((WIDE, 256), F32)

    key_top = jnp.max(squares(k_s[0], spread), axis=0, keepdims=True)
    for n in range(1, shards):
        key_top = jnp.maximum(key_top, jnp.max(squares(k_s[n], spread), axis=0, keepdims=True))
    if not first:
        for n in range(SUFFIX):
            top = jnp.max(squares(ks_s[n], spread), axis=0, keepdims=True)
            key_top = jnp.maximum(key_top, top)

    query_top = jnp.max(squares(q_s[...], spread), axis=0, keepdims=True)
    fast = (jnp.max(query_top * key_top) < BOUND * BOUND / 1.05).astype(jnp.int32)
    if not first:
        fast = fast * fast_in[0]
    for c in late:
        c.wait()

    owner_of = [owners[line + 2 * ((ring + s) % DEPTH)] for s in shifts]

    def stacked(row, s):
        cols = slice(128 * s, 128 * s + 128)
        q = q_s[pl.ds(row, TILE), cols]
        zero = jnp.zeros_like(q)
        return jnp.concatenate([jnp.where(low, q, zero), jnp.where(low, zero, q)], axis=0)

    def by_head(pair):
        return jnp.where(low, pair[:TILE], pair[TILE:])

    def four(stack):
        rows = [stack[TILE * h : TILE * h + TILE] for h in range(4)]
        upper = jnp.where(wide_head == 2, rows[2], rows[3])
        return jnp.where(wide_head == 0, rows[0], jnp.where(wide_head == 1, rows[1], upper))

    def step_fast(row, keys, values, ok, mask):
        q = q_s[pl.ds(row, TILE), :]
        zero = jnp.zeros_like(q)
        stack = jnp.concatenate([jnp.where(wide_head == h, q, zero) for h in range(4)], axis=0)
        weights = jnp.exp(nt_dot(stack, keys[...]))
        if mask is not None:
            weights = jnp.where(jnp.concatenate([mask] * 4, axis=0), weights, 0.0)
        sums = weights[:, 0:128]
        for n in range(1, keys.shape[0] // 128):
            sums = sums + weights[:, 128 * n : 128 * n + 128]
        sums = jnp.sum(sums, axis=1, keepdims=True)
        part = dot(weights.astype(BF), values[...])
        acc[pl.ds(row, TILE), :] += jnp.where(ok, four(part), 0.0)
        total[pl.ds(row, TILE), :] += jnp.where(ok, four(sums), 0.0)

    def step_slow(row, keys, values, ok, mask):
        for s in range(2):
            cols = slice(128 * s, 128 * s + 128)
            scores = nt_dot(stacked(row, s), keys[:, cols])
            if mask is not None:
                mask2 = jnp.concatenate([mask, mask], axis=0)
                scores = jnp.where(mask2, scores, NEG)
            top = jnp.max(scores, axis=1, keepdims=True)
            before = total[pl.ds(row, TILE), cols]
            old = jnp.where(before > 0.0, shift_s[pl.ds(row, TILE), cols], NEG)
            tops = by_head(jnp.broadcast_to(top, (2 * TILE, 128)))
            new = jnp.where(ok, jnp.maximum(old, tops), old)
            used = jnp.concatenate([new[:, 0:1], new[:, 64:65]], axis=0)
            ok2 = jnp.concatenate([ok, ok], axis=0)
            weights = jnp.exp(scores - jnp.where(ok2, used, top))
            if mask is not None:
                weights = jnp.where(mask2, weights, 0.0)
            part = dot(weights.astype(BF), values[:, cols])
            sums = jnp.sum(weights, axis=1, keepdims=True)
            sums = jnp.broadcast_to(sums, (2 * TILE, 128))
            fade = jnp.exp(old - new)
            acc[pl.ds(row, TILE), cols] = acc[pl.ds(row, TILE), cols] * fade + jnp.where(
                ok, by_head(part), 0.0
            )
            total[pl.ds(row, TILE), cols] = before * fade + jnp.where(ok, by_head(sums), 0.0)
            shift_s[pl.ds(row, TILE), cols] = jnp.where(ok, new, shift_s[pl.ds(row, TILE), cols])

    def tile_step(t, request):
        row = pl.multiple_of(t * TILE, TILE)
        member = t * TILE // ROWS
        block = (member // 2) * 8 + ring * 2 + member % 2
        token0 = block * ROWS + (t * TILE) % ROWS
        if first:
            acc[pl.ds(row, TILE), :] = jnp.zeros((TILE, 256), F32)
            total[pl.ds(row, TILE), :] = jnp.zeros((TILE, 256), F32)

            @pl.when(fast == 0)
            def _():
                shift_s[pl.ds(row, TILE), :] = jnp.zeros((TILE, 256), F32)

        request = lax.while_loop(lambda r: starts[r + 1] <= token0, lambda r: r + 1, request)
        token = token0 + lax.broadcasted_iota(jnp.int32, (TILE, 1), 0)

        def more(c):
            r = c[0]
            return (r < REQS) & (starts[jnp.minimum(r, REQS)] < token0 + TILE)

        def visit(c):
            r, bits, group, start = c
            here = token >= starts[r]
            g = groups[r]
            return (
                r + 1,
                bits | (jnp.int32(1) << g),
                jnp.where(here, g, group),
                jnp.where(here, starts[r], start),
            )

        zeros = jnp.zeros((TILE, 1), jnp.int32)
        _, bits, group, start = lax.while_loop(more, visit, (request, jnp.int32(0), zeros, zeros))

        def shard(j, _):
            g = owner_of[0]
            for n in range(1, shards):
                g = jnp.where(j == n, owner_of[n], g)
            here = (bits >> g) & 1

            @pl.when((here == 1) & (fast == 1))
            def _():
                step_fast(row, k_s.at[j], v_s.at[j], group == g, None)

            @pl.when((here == 1) & (fast == 0))
            def _():
                step_slow(row, k_s.at[j], v_s.at[j], group == g, None)

            return 0

        lax.fori_loop(0, shards, shard, 0)
        if not first:

            def suffix(j, _):
                key0 = (line + 2 * ((ring - j + DEPTH) % DEPTH)) * ROWS
                here = (key0 < token0 + TILE) & (starts[request] < key0 + ROWS)

                def args():
                    key = key0 + lax.broadcasted_iota(jnp.int32, (TILE, ROWS), 1)
                    mask = (key >= start) & (key <= token)
                    ok = (start < key0 + ROWS) & (key0 <= token)
                    return row, ks_s.at[j], vs_s.at[j], ok, mask

                @pl.when(here & (fast == 1))
                def _():
                    step_fast(*args())

                @pl.when(here & (fast == 0))
                def _():
                    step_slow(*args())

                return 0

            lax.fori_loop(0, SUFFIX, suffix, 0)
        else:
            for c in leave(t):
                c.start()
        return request

    def leave(t):
        rows = pl.ds(pl.multiple_of(t * TILE, TILE), TILE)
        return (
            pltpu.make_async_copy(acc.at[rows, :], acc_out.at[rows, :], sem.at[0]),
            pltpu.make_async_copy(total.at[rows, :], total_out.at[rows, :], sem.at[1]),
        )

    lax.fori_loop(0, TILES, tile_step, jnp.int32(0))

    if first:
        fast_ref[0] = fast

        @pl.when(fast == 0)
        def _():
            moved = pltpu.make_async_copy(shift_s, ref_out, sem.at[2])
            moved.start()
            moved.wait()

        pltpu.make_async_copy(acc, acc_out, sem.at[0]).wait()
        pltpu.make_async_copy(total, total_out, sem.at[1]).wait()
    else:

        def finish(b, _):
            for u in range(2):
                row = pl.multiple_of(b * ROWS + u * TILE, TILE)
                lses = []
                for s in range(2):
                    cols = slice(128 * s, 128 * s + 128)
                    summed = total[pl.ds(row, TILE), cols]
                    some = summed > 0.0
                    safe = jnp.where(some, summed, 1.0)
                    part = jnp.where(some, acc[pl.ds(row, TILE), cols] / safe, 0.0)
                    out_ref[b, u * TILE : (u + 1) * TILE, cols] = part.astype(BF)
                    lses.append(
                        jnp.where(some, shift_s[pl.ds(row, TILE), cols] + jnp.log(safe), F32(NEG))
                    )
                flat = jnp.transpose(jnp.where(lane % HD < HD // 2, lses[0], lses[1]))
                rows4 = jnp.concatenate([flat[r : r + 1, :] for r in (0, 64, 32, 96)], axis=0)
                high = rows4.astype(BF).astype(F32)
                mid = (rows4 - high).astype(BF).astype(F32)
                rest4 = rows4 - high - mid
                stats = jnp.concatenate([high, mid, rest4, jnp.zeros_like(high)], axis=0)
                out_ref[b, ROWS : ROWS + STATS, u * TILE : (u + 1) * TILE] = stats.astype(BF)
            return 0

        lax.fori_loop(0, PLANE, finish, 0)


def attend(first, shifts, scalars, flags, q, kvs, extra):
    shards = len(shifts)
    blocks = 1 if first else SUFFIX
    state = jax.ShapeDtypeStruct((WIDE, 256), F32)
    scratch = [
        pltpu.VMEM((WIDE, 256), F32),
        pltpu.VMEM((WIDE, 256), F32),
        pltpu.VMEM((WIDE, 256), F32),
        pltpu.VMEM((WIDE, 256), BF),
        pltpu.VMEM((shards, PFX, 256), BF),
        pltpu.VMEM((shards, PFX, 256), BF),
        pltpu.VMEM((blocks, ROWS, 256), BF),
        pltpu.VMEM((blocks, ROWS, 256), BF),
        pltpu.SMEM((REQS + 1,), jnp.int32),
        pltpu.SemaphoreType.DMA((16,)),
    ]
    if first:
        out_shape = (state, state, state, jax.ShapeDtypeStruct((1,), jnp.int32))
        out_specs = (anywhere(), anywhere(), anywhere(), smem())
    else:
        out_shape = jax.ShapeDtypeStruct((PLANE, ROWS + STATS, 256), BF)
        out_specs = whole()
    small = list(scalars) + list(flags)
    operands = [q.reshape(WIDE, 256)] + list(kvs) + list(extra)
    return pl.pallas_call(
        functools.partial(attend_kernel, first, shifts),
        out_shape=out_shape,
        in_specs=[smem()] * len(small) + [anywhere()] * len(operands),
        out_specs=out_specs,
        scratch_shapes=scratch,
        compiler_params=params(),
        name="attend_first" if first else "attend_rest",
    )(*small, *operands)


def merge_kernel(parts_ref, weight_ref, keep_ref, give_ref, out_ref):
    rows = []
    for i in range(PLANE):
        st = parts_ref[i, ROWS : ROWS + STATS, :].astype(F32)
        rows.append(st[0:4] + st[4:8] + st[8:12])
    top = functools.reduce(jnp.maximum, rows)
    rows = [jnp.exp(r - top) for r in rows]
    total = functools.reduce(jnp.add, rows)
    weights = jnp.concatenate([r / total for r in rows], axis=0)
    weights = jnp.concatenate([weights, jnp.zeros((128 - 4 * PLANE, ROWS), F32)], axis=0)
    tall = jnp.transpose(weights)
    high = tall.astype(BF)
    rest = (tall - high.astype(F32)).astype(BF)
    both = jnp.concatenate([high, rest], axis=1)
    source = lax.broadcasted_iota(jnp.int32, (256, 256), 0) % 128
    column_head = lax.broadcasted_iota(jnp.int32, (256, 256), 1) // HD
    acc = jnp.zeros((ROWS, 256), F32)
    for i in range(PLANE):
        spread = (source == column_head + 4 * i).astype(F32).astype(BF)
        acc = acc + dot(both, spread) * parts_ref[i, 0:ROWS, :].astype(F32)
    out_ref[...] = acc.astype(BF)
    half = ROWS // 2
    core = lax.axis_index("tp") % 2
    keep_row = pl.multiple_of(core * half, half)
    give_row = pl.multiple_of((1 - core) * half, half)
    give_ref[...] = dot(out_ref[pl.ds(give_row, half), :], weight_ref[...])
    keep_ref[...] = dot(out_ref[pl.ds(keep_row, half), :], weight_ref[...])


def merge(parts, weight):
    half = jax.ShapeDtypeStruct((ROWS // 2, 1024), F32)
    return pl.pallas_call(
        merge_kernel,
        out_shape=(half, half),
        in_specs=[whole()] * 2,
        out_specs=(whole(), whole()),
        scratch_shapes=[pltpu.VMEM((ROWS, 256), BF)],
        compiler_params=params(),
        name="merge",
    )(parts, weight)


def normalize(values, gain, shift):
    center = values - jnp.mean(values, axis=-1, keepdims=True)
    spread = jnp.mean(center * center, axis=-1, keepdims=True)
    return center * lax.rsqrt(spread + 1e-05) * gain + shift


def middle_kernel(
    up_own, up_mate, down_own, down_mate, mine, theirs, hidden_ref,
    out_bias, gain, shift, bias_own, bias_mate, normed_ref, part_ref, up_s, down_s, sem,
):
    copies = [
        pltpu.make_async_copy(up_own, up_s.at[0], sem.at[0]),
        pltpu.make_async_copy(up_mate, up_s.at[1], sem.at[1]),
        pltpu.make_async_copy(down_own, down_s.at[0], sem.at[2]),
        pltpu.make_async_copy(down_mate, down_s.at[1], sem.at[3]),
    ]
    for c in copies:
        c.start()
    half = ROWS // 2
    row = pl.multiple_of((lax.axis_index("tp") % 2) * half, half)
    hidden = hidden_ref[pl.ds(row, half), :].astype(F32)
    mixed = (mine[...].astype(F32) + theirs[...].astype(F32)) + out_bias[...] + hidden
    normed = normalize(mixed, gain[0:1, :], shift[0:1, :]).astype(BF)
    normed_ref[...] = normed
    total = None
    biases = (bias_own, bias_mate)
    for n in range(2):
        copies[n].wait()
        copies[2 + n].wait()
        for c in range(4):
            cols = slice(256 * c, 256 * c + 256)
            up = dot(normed, up_s[n, :, cols]) + biases[n][:, cols]
            inner = (0.5 * up * (1.0 + lax.erf(up * F32(0.7071067811865476)))).astype(BF)
            piece = dot(inner, down_s[n, cols, :])
            total = piece if total is None else total + piece
    part_ref[...] = total.astype(BF)


def middle(weights, mine, theirs, hidden, out_bias, gain, shift, bias_own, bias_mate):
    half = ROWS // 2
    return pl.pallas_call(
        middle_kernel,
        out_shape=(
            jax.ShapeDtypeStruct((half, 1024), BF),
            jax.ShapeDtypeStruct((half, 1024), BF),
        ),
        in_specs=[anywhere()] * 4 + [whole()] * 8,
        out_specs=(whole(), whole()),
        scratch_shapes=[
            pltpu.VMEM((2, 1024, 1024), BF),
            pltpu.VMEM((2, 1024, 1024), BF),
            pltpu.SemaphoreType.DMA((4,)),
        ],
        compiler_params=params(),
        name="middle",
    )(*weights, mine, theirs, hidden, out_bias, gain, shift, bias_own, bias_mate)


def final_kernel(own, other, normed, bias, gain, shift, out_ref):
    lowered = own[...].astype(F32) + other[...].astype(F32)
    total = lowered + bias[...] + normed[...].astype(F32)
    out_ref[...] = normalize(total, gain[1:2, :], shift[1:2, :]).astype(BF)


def final(own, other, normed, bias, gain, shift):
    return pl.pallas_call(
        final_kernel,
        out_shape=jax.ShapeDtypeStruct(own.shape, BF),
        in_specs=[whole()] * 6,
        out_specs=whole(),
        compiler_params=params(),
        name="final",
    )(own, other, normed, bias, gain, shift)


def from_ring(value, by):
    pairs = [
        (z * 8 + ((x + by) % DEPTH) * 2 + y, z * 8 + x * 2 + y)
        for z in range(4)
        for x in range(DEPTH)
        for y in range(2)
    ]
    return lax.ppermute(value, "seq", pairs)


def from_tp(value, flip):
    return lax.ppermute(value, "tp", [(i, i ^ flip) for i in range(4)])


def shards(
    hidden_in, query_weight, query_bias, keyval_weight, keyval_bias, out_weight, out_bias,
    up_weight, up_bias, down_weight, down_bias, norm_gain, norm_bias, prefix_keys,
    prefix_values, suffix_lengths, request_group, owner_group,
):
    core = lax.axis_index("tp") % 2
    k_up, v_up = from_ring(prefix_keys, 1), from_ring(prefix_values, 1)
    k_down, v_down = from_ring(prefix_keys, 3), from_ring(prefix_values, 3)
    k_far, v_far = from_ring(k_up, 1), from_ring(v_down, 3)
    q_copies, own_suffix = project(hidden_in, query_weight, query_bias, keyval_weight, keyval_bias)
    back_suffix, back_two = from_ring(own_suffix, 3), from_ring(own_suffix, 2)
    queries = lax.all_to_all(q_copies, "seq", 0, 0, tiled=True, axis_index_groups=SEQ_PLANES)
    scalars = (suffix_lengths, request_group, owner_group)
    acc, total, shift, fast = attend(
        True,
        (0, 1, 3),
        scalars,
        (),
        queries,
        (prefix_keys, prefix_values, k_up, v_up, k_down, v_down),
        (),
    )
    parts = attend(
        False,
        (2,),
        scalars,
        (fast,),
        queries,
        (k_far, v_far),
        (own_suffix, back_suffix, back_two, acc, total, shift),
    )
    parts = lax.all_to_all(parts, "seq", 0, 0, tiled=True, axis_index_groups=SEQ_PLANES)
    up_mate = from_tp(up_weight, 1)
    down_mate = from_tp(down_weight, 1)
    bias_mate = from_tp(up_bias.reshape(1, -1), 1)
    keep, give = merge(parts, out_weight)
    mine = (keep + from_tp(give, 1)).astype(BF)
    normed, part = middle(
        (up_weight, up_mate, down_weight, down_mate),
        mine,
        from_tp(mine, 2),
        hidden_in,
        out_bias.reshape(1, -1),
        norm_gain,
        norm_bias,
        up_bias.reshape(1, -1),
        bias_mate,
    )
    result = final(part, from_tp(part, 2), normed, down_bias.reshape(1, -1), norm_gain, norm_bias)
    other = from_tp(result, 1)
    own_half = lax.broadcasted_iota(jnp.int32, (2, 1, 1), 0) == core
    return jnp.where(own_half, result[None], other[None]).reshape(ROWS, result.shape[1])


def solution(mesh):
    return jax.shard_map(
        shards,
        mesh=mesh,
        in_specs=(
            P("seq", None),
            P(None, "tp"),
            P("tp"),
            P(None, None, "tp"),
            P(None, "tp"),
            P("tp", None),
            P(),
            P(None, "tp"),
            P("tp"),
            P("tp", None),
            P(),
            P(),
            P(),
            P("seq", "tp"),
            P("seq", "tp"),
            P(),
            P(),
            P(),
        ),
        out_specs=P("seq", None),
        check_vma=False,
    )
```

```python
import functools

import jax
import jax.numpy as jnp
from jax import lax
from jax.experimental import pallas as pl
from jax.experimental.pallas import tpu as pltpu
from jax.sharding import PartitionSpec as P

BF = jnp.bfloat16
F32 = jnp.float32
NEG = -1e30
HD = 64
ROWS = 256
PLANE = 8
DEPTH = 4
SUFFIX = 3
TILE = 128
PFX = 1024
TOKENS = 8192
REQS = 48
STATS = 16
VMEM_BYTES = 60 * 1024 * 1024

SEQ_PLANES = [[z * 8 + x * 2 + y for z in range(4) for y in range(2)] for x in range(DEPTH)]


def params(semantics=None):
    return pltpu.CompilerParams(vmem_limit_bytes=VMEM_BYTES, dimension_semantics=semantics)


def whole():
    return pl.BlockSpec(memory_space=pltpu.VMEM)


def anywhere():
    return pl.BlockSpec(memory_space=pl.ANY)


def smem():
    return pl.BlockSpec(memory_space=pltpu.SMEM)


def nt_dot(left, right):
    return lax.dot_general(left, right, (((1,), (1,)), ((), ())), preferred_element_type=F32)


def dot(left, right):
    return jnp.dot(left, right, preferred_element_type=F32)


def project_kernel(x_ref, wq_ref, bq_ref, wkv_ref, bkv_ref, q_ref, kv_ref):
    x = x_ref[...]
    q = (dot(x, wq_ref[...]) + bq_ref[...]).astype(BF) * BF(0.125)
    for n in range(PLANE):
        q_ref[n] = q
    for n in range(2):
        kv_ref[n] = (dot(x, wkv_ref[n]) + bkv_ref[n : n + 1, :]).astype(BF)


def project(x, wq, bq, wkv, bkv):
    cols = wq.shape[1]
    return pl.pallas_call(
        project_kernel,
        out_shape=(
            jax.ShapeDtypeStruct((PLANE, ROWS, cols), BF),
            jax.ShapeDtypeStruct((2, ROWS, cols), BF),
        ),
        in_specs=[whole()] * 5,
        out_specs=(whole(), whole()),
        compiler_params=params(),
        name="project",
    )(x, wq, bq.reshape(1, cols), wkv, bkv)


BOUND = 70.0
WIDE = PLANE * ROWS
TILES = WIDE // TILE


def squares(rows, spread):
    wide = rows.astype(F32)
    return dot((wide * wide).astype(BF), spread)


def attend_kernel(first, shifts, *refs):
    shards = len(shifts)
    lengths, groups, owners = refs[:3]
    refs = refs[3:]
    if first:
        q_hbm, own_k, own_v, kv_up, kv_down = refs[:5]
        kv_hbm = (own_k, own_v, kv_up.at[0], kv_up.at[1], kv_down.at[0], kv_down.at[1])
        refs = refs[5:]
        acc_out, total_out, ref_out, fast_ref = refs[:4]
        refs = refs[4:]
    else:
        fast_in = refs[0]
        q_hbm = refs[1]
        far_k, far_bundle, own_suffix, back_two = refs[2:6]
        acc_in, total_in, ref_in, out_ref = refs[6:10]
        refs = refs[10:]
        kv_hbm = (far_k, far_bundle.at[0:PFX])
        suffixes = (
            (own_suffix.at[0], own_suffix.at[1]),
            (far_bundle.at[PFX : PFX + ROWS], far_bundle.at[PFX + ROWS : PFX + 2 * ROWS]),
            (back_two.at[0], back_two.at[1]),
        )
    acc, total, shift_s, q_s, k_s, v_s, ks_s, vs_s, starts, sem = refs

    place = lax.axis_index("seq")
    ring = (place // 2) % DEPTH
    line = place - 2 * ring

    early = [pltpu.make_async_copy(q_hbm, q_s, sem.at[0])]
    late = []
    for n in range(shards):
        early.append(pltpu.make_async_copy(kv_hbm[2 * n], k_s.at[n], sem.at[1 + 2 * n]))
        late.append(pltpu.make_async_copy(kv_hbm[2 * n + 1], v_s.at[n], sem.at[2 + 2 * n]))
    n_sem = 1 + 2 * shards
    if not first:
        for n in range(SUFFIX):
            early.append(pltpu.make_async_copy(suffixes[n][0], ks_s.at[n], sem.at[n_sem]))
            late.append(pltpu.make_async_copy(suffixes[n][1], vs_s.at[n], sem.at[n_sem + 1]))
            n_sem += 2
        late.append(pltpu.make_async_copy(acc_in, acc, sem.at[n_sem]))
        late.append(pltpu.make_async_copy(total_in, total, sem.at[n_sem + 1]))
        n_sem += 2
    for c in early + late:
        c.start()

    def add_start(r, done):
        starts[r] = done
        return done + lengths[r]

    starts[REQS] = lax.fori_loop(0, REQS, add_start, jnp.int32(0))

    lane = lax.broadcasted_iota(jnp.int32, (TILE, 128), 1)
    low = lane < HD
    wide_head = lax.broadcasted_iota(jnp.int32, (TILE, 256), 1) // HD
    row_head = lax.broadcasted_iota(jnp.int32, (256, 128), 0) // HD
    spread = (row_head == lax.broadcasted_iota(jnp.int32, (256, 128), 1)).astype(F32).astype(BF)
    for c in early:
        c.wait()

    if not first:
        moved = pltpu.make_async_copy(ref_in, shift_s, sem.at[n_sem])
        slow_before = 1 - fast_in[0]

        @pl.when(slow_before > 0)
        def _():
            moved.start()
            moved.wait()

        @pl.when(slow_before == 0)
        def _():
            shift_s[...] = jnp.zeros((WIDE, 256), F32)

    key_top = jnp.max(squares(k_s[0], spread), axis=0, keepdims=True)
    for n in range(1, shards):
        key_top = jnp.maximum(key_top, jnp.max(squares(k_s[n], spread), axis=0, keepdims=True))
    if not first:
        for n in range(SUFFIX):
            top = jnp.max(squares(ks_s[n], spread), axis=0, keepdims=True)
            key_top = jnp.maximum(key_top, top)

    query_top = jnp.max(squares(q_s[...], spread), axis=0, keepdims=True)
    fast = (jnp.max(query_top * key_top) < BOUND * BOUND / 1.05).astype(jnp.int32)
    if not first:
        fast = fast * fast_in[0]
    for c in late:
        c.wait()

    owner_of = [owners[line + 2 * ((ring + s) % DEPTH)] for s in shifts]

    def stacked(row, s):
        cols = slice(128 * s, 128 * s + 128)
        q = q_s[pl.ds(row, TILE), cols]
        zero = jnp.zeros_like(q)
        return jnp.concatenate([jnp.where(low, q, zero), jnp.where(low, zero, q)], axis=0)

    def by_head(pair):
        return jnp.where(low, pair[:TILE], pair[TILE:])

    def four(stack):
        rows = [stack[TILE * h : TILE * h + TILE] for h in range(4)]
        upper = jnp.where(wide_head == 2, rows[2], rows[3])
        return jnp.where(wide_head == 0, rows[0], jnp.where(wide_head == 1, rows[1], upper))

    def step_fast(row, keys, values, ok, mask):
        q = q_s[pl.ds(row, TILE), :]
        zero = jnp.zeros_like(q)
        stack = jnp.concatenate([jnp.where(wide_head == h, q, zero) for h in range(4)], axis=0)
        weights = jnp.exp(nt_dot(stack, keys[...]))
        if mask is not None:
            weights = jnp.where(jnp.concatenate([mask] * 4, axis=0), weights, 0.0)
        sums = weights[:, 0:128]
        for n in range(1, keys.shape[0] // 128):
            sums = sums + weights[:, 128 * n : 128 * n + 128]
        sums = jnp.sum(sums, axis=1, keepdims=True)
        part = dot(weights.astype(BF), values[...])
        acc[pl.ds(row, TILE), :] += jnp.where(ok, four(part), 0.0)
        total[pl.ds(row, TILE), :] += jnp.where(ok, four(sums), 0.0)

    def step_slow(row, keys, values, ok, mask):
        for s in range(2):
            cols = slice(128 * s, 128 * s + 128)
            scores = nt_dot(stacked(row, s), keys[:, cols])
            if mask is not None:
                mask2 = jnp.concatenate([mask, mask], axis=0)
                scores = jnp.where(mask2, scores, NEG)
            top = jnp.max(scores, axis=1, keepdims=True)
            before = total[pl.ds(row, TILE), cols]
            old = jnp.where(before > 0.0, shift_s[pl.ds(row, TILE), cols], NEG)
            tops = by_head(jnp.broadcast_to(top, (2 * TILE, 128)))
            new = jnp.where(ok, jnp.maximum(old, tops), old)
            used = jnp.concatenate([new[:, 0:1], new[:, 64:65]], axis=0)
            ok2 = jnp.concatenate([ok, ok], axis=0)
            weights = jnp.exp(scores - jnp.where(ok2, used, top))
            if mask is not None:
                weights = jnp.where(mask2, weights, 0.0)
            part = dot(weights.astype(BF), values[:, cols])
            sums = jnp.sum(weights, axis=1, keepdims=True)
            sums = jnp.broadcast_to(sums, (2 * TILE, 128))
            fade = jnp.exp(old - new)
            acc[pl.ds(row, TILE), cols] = acc[pl.ds(row, TILE), cols] * fade + jnp.where(
                ok, by_head(part), 0.0
            )
            total[pl.ds(row, TILE), cols] = before * fade + jnp.where(ok, by_head(sums), 0.0)
            shift_s[pl.ds(row, TILE), cols] = jnp.where(ok, new, shift_s[pl.ds(row, TILE), cols])

    def tile_step(t, request):
        row = pl.multiple_of(t * TILE, TILE)
        member = t * TILE // ROWS
        block = (member // 2) * 8 + ring * 2 + member % 2
        token0 = block * ROWS + (t * TILE) % ROWS
        if first:
            acc[pl.ds(row, TILE), :] = jnp.zeros((TILE, 256), F32)
            total[pl.ds(row, TILE), :] = jnp.zeros((TILE, 256), F32)

            @pl.when(fast == 0)
            def _():
                shift_s[pl.ds(row, TILE), :] = jnp.zeros((TILE, 256), F32)

        request = lax.while_loop(lambda r: starts[r + 1] <= token0, lambda r: r + 1, request)
        token = token0 + lax.broadcasted_iota(jnp.int32, (TILE, 1), 0)

        def more(c):
            r = c[0]
            return (r < REQS) & (starts[jnp.minimum(r, REQS)] < token0 + TILE)

        def visit(c):
            r, bits, group, start = c
            here = token >= starts[r]
            g = groups[r]
            return (
                r + 1,
                bits | (jnp.int32(1) << g),
                jnp.where(here, g, group),
                jnp.where(here, starts[r], start),
            )

        zeros = jnp.zeros((TILE, 1), jnp.int32)
        _, bits, group, start = lax.while_loop(more, visit, (request, jnp.int32(0), zeros, zeros))

        def shard(j, _):
            g = owner_of[0]
            for n in range(1, shards):
                g = jnp.where(j == n, owner_of[n], g)
            here = (bits >> g) & 1

            @pl.when((here == 1) & (fast == 1))
            def _():
                step_fast(row, k_s.at[j], v_s.at[j], group == g, None)

            @pl.when((here == 1) & (fast == 0))
            def _():
                step_slow(row, k_s.at[j], v_s.at[j], group == g, None)

            return 0

        lax.fori_loop(0, shards, shard, 0)
        if not first:

            def suffix(j, _):
                key0 = (line + 2 * ((ring - j + DEPTH) % DEPTH)) * ROWS
                here = (key0 < token0 + TILE) & (starts[request] < key0 + ROWS)

                def args():
                    key = key0 + lax.broadcasted_iota(jnp.int32, (TILE, ROWS), 1)
                    mask = (key >= start) & (key <= token)
                    ok = (start < key0 + ROWS) & (key0 <= token)
                    return row, ks_s.at[j], vs_s.at[j], ok, mask

                @pl.when(here & (fast == 1))
                def _():
                    step_fast(*args())

                @pl.when(here & (fast == 0))
                def _():
                    step_slow(*args())

                return 0

            lax.fori_loop(0, SUFFIX, suffix, 0)
        else:
            for c in leave(t):
                c.start()
        return request

    def leave(t):
        rows = pl.ds(pl.multiple_of(t * TILE, TILE), TILE)
        return (
            pltpu.make_async_copy(acc.at[rows, :], acc_out.at[rows, :], sem.at[0]),
            pltpu.make_async_copy(total.at[rows, :], total_out.at[rows, :], sem.at[1]),
        )

    lax.fori_loop(0, TILES, tile_step, jnp.int32(0))

    if first:
        fast_ref[0] = fast

        @pl.when(fast == 0)
        def _():
            moved = pltpu.make_async_copy(shift_s, ref_out, sem.at[2])
            moved.start()
            moved.wait()

        pltpu.make_async_copy(acc, acc_out, sem.at[0]).wait()
        pltpu.make_async_copy(total, total_out, sem.at[1]).wait()
    else:

        def finish(b, _):
            for u in range(2):
                row = pl.multiple_of(b * ROWS + u * TILE, TILE)
                lses = []
                for s in range(2):
                    cols = slice(128 * s, 128 * s + 128)
                    summed = total[pl.ds(row, TILE), cols]
                    some = summed > 0.0
                    safe = jnp.where(some, summed, 1.0)
                    part = jnp.where(some, acc[pl.ds(row, TILE), cols] / safe, 0.0)
                    out_ref[b, u * TILE : (u + 1) * TILE, cols] = part.astype(BF)
                    lses.append(
                        jnp.where(some, shift_s[pl.ds(row, TILE), cols] + jnp.log(safe), F32(NEG))
                    )
                flat = jnp.transpose(jnp.where(lane % HD < HD // 2, lses[0], lses[1]))
                rows4 = jnp.concatenate([flat[r : r + 1, :] for r in (0, 64, 32, 96)], axis=0)
                high = rows4.astype(BF).astype(F32)
                mid = (rows4 - high).astype(BF).astype(F32)
                rest4 = rows4 - high - mid
                stats = jnp.concatenate([high, mid, rest4, jnp.zeros_like(high)], axis=0)
                out_ref[b, ROWS : ROWS + STATS, u * TILE : (u + 1) * TILE] = stats.astype(BF)
            return 0

        lax.fori_loop(0, PLANE, finish, 0)


def attend(first, shifts, scalars, flags, q, kvs, extra):
    shards = len(shifts)
    blocks = 1 if first else SUFFIX
    state = jax.ShapeDtypeStruct((WIDE, 256), F32)
    scratch = [
        pltpu.VMEM((WIDE, 256), F32),
        pltpu.VMEM((WIDE, 256), F32),
        pltpu.VMEM((WIDE, 256), F32),
        pltpu.VMEM((WIDE, 256), BF),
        pltpu.VMEM((shards, PFX, 256), BF),
        pltpu.VMEM((shards, PFX, 256), BF),
        pltpu.VMEM((blocks, ROWS, 256), BF),
        pltpu.VMEM((blocks, ROWS, 256), BF),
        pltpu.SMEM((REQS + 1,), jnp.int32),
        pltpu.SemaphoreType.DMA((16,)),
    ]
    if first:
        out_shape = (state, state, state, jax.ShapeDtypeStruct((1,), jnp.int32))
        out_specs = (anywhere(), anywhere(), anywhere(), smem())
    else:
        out_shape = jax.ShapeDtypeStruct((PLANE, ROWS + STATS, 256), BF)
        out_specs = whole()
    small = list(scalars) + list(flags)
    operands = [q.reshape(WIDE, 256)] + list(kvs) + list(extra)
    return pl.pallas_call(
        functools.partial(attend_kernel, first, shifts),
        out_shape=out_shape,
        in_specs=[smem()] * len(small) + [anywhere()] * len(operands),
        out_specs=out_specs,
        scratch_shapes=scratch,
        compiler_params=params(),
        cost_estimate=pl.CostEstimate(
            flops=shards * 8_000_000_000, transcendentals=0, bytes_accessed=16_000_000
        ),
        name="attend_first" if first else "attend_rest",
    )(*small, *operands)


def merge_kernel(parts_ref, keep_ref, give_ref, out_ref):
    rows = []
    for i in range(PLANE):
        st = parts_ref[i, ROWS : ROWS + STATS, :].astype(F32)
        rows.append(st[0:4] + st[4:8] + st[8:12])
    top = functools.reduce(jnp.maximum, rows)
    rows = [jnp.exp(r - top) for r in rows]
    total = functools.reduce(jnp.add, rows)
    weights = jnp.concatenate([r / total for r in rows], axis=0)
    weights = jnp.concatenate([weights, jnp.zeros((128 - 4 * PLANE, ROWS), F32)], axis=0)
    tall = jnp.transpose(weights)
    high = tall.astype(BF)
    rest = (tall - high.astype(F32)).astype(BF)
    both = jnp.concatenate([high, rest], axis=1)
    source = lax.broadcasted_iota(jnp.int32, (256, 256), 0) % 128
    column_head = lax.broadcasted_iota(jnp.int32, (256, 256), 1) // HD
    acc = jnp.zeros((ROWS, 256), F32)
    for i in range(PLANE):
        spread = (source == column_head + 4 * i).astype(F32).astype(BF)
        acc = acc + dot(both, spread) * parts_ref[i, 0:ROWS, :].astype(F32)
    out_ref[...] = acc
    half = ROWS // 2
    core = lax.axis_index("tp") % 2
    keep_row = pl.multiple_of(core * half, half)
    give_row = pl.multiple_of((1 - core) * half, half)
    give_ref[...] = out_ref[pl.ds(give_row, half), :].astype(BF)
    keep_ref[...] = out_ref[pl.ds(keep_row, half), :].astype(BF)


def merge(parts):
    half = jax.ShapeDtypeStruct((ROWS // 2, 256), BF)
    return pl.pallas_call(
        merge_kernel,
        out_shape=(half, half),
        in_specs=[whole()],
        out_specs=(whole(), whole()),
        scratch_shapes=[pltpu.VMEM((ROWS, 256), F32)],
        compiler_params=params(),
        name="merge",
    )(parts)


def normalize(values, gain, shift):
    center = values - jnp.mean(values, axis=-1, keepdims=True)
    spread = jnp.mean(center * center, axis=-1, keepdims=True)
    return center * lax.rsqrt(spread + 1e-05) * gain + shift


def middle_kernel(
    up_own, up_mate, down_own, down_mate, ow_0, ow_1, ow_2, ow_3, mine, mate, across, corner, hidden_ref,
    out_bias, gain, shift, bias_own, bias_mate, normed_ref, part_ref,
    up_s, down_s, out_s, a_s, sem,
):
    place = lax.axis_index("tp")
    core = place % 2
    other = 1 - core
    side = place - core
    far = 2 - side
    copies = [
        pltpu.make_async_copy(mine, a_s.at[side + core], sem.at[0]),
        pltpu.make_async_copy(mate, a_s.at[side + other], sem.at[1]),
        pltpu.make_async_copy(across, a_s.at[far + core], sem.at[2]),
        pltpu.make_async_copy(corner, a_s.at[far + other], sem.at[3]),
        pltpu.make_async_copy(ow_0, out_s.at[side + core], sem.at[4]),
        pltpu.make_async_copy(ow_1, out_s.at[side + other], sem.at[9]),
        pltpu.make_async_copy(ow_2, out_s.at[far + core], sem.at[10]),
        pltpu.make_async_copy(ow_3, out_s.at[far + other], sem.at[11]),
        pltpu.make_async_copy(up_own, up_s.at[0], sem.at[5]),
        pltpu.make_async_copy(up_mate, up_s.at[1], sem.at[6]),
        pltpu.make_async_copy(down_own, down_s.at[0], sem.at[7]),
        pltpu.make_async_copy(down_mate, down_s.at[1], sem.at[8]),
    ]
    for c in copies:
        c.start()
    half = ROWS // 2
    row = pl.multiple_of(core * half, half)
    for c in copies[:8]:
        c.wait()
    mixed = out_bias[...] + hidden_ref[pl.ds(row, half), :].astype(F32)
    attended = jnp.concatenate([a_s[n] for n in range(4)], axis=1)
    mixed = mixed + dot(attended, out_s[...].reshape(1024, 1024))
    normed = normalize(mixed, gain[0:1, :], shift[0:1, :]).astype(BF)
    normed_ref[...] = normed
    total = None
    biases = (bias_own, bias_mate)
    for n in range(2):
        copies[8 + n].wait()
        copies[10 + n].wait()
        for c in range(4):
            cols = slice(256 * c, 256 * c + 256)
            up = dot(normed, up_s[n, :, cols]) + biases[n][:, cols]
            inner = (0.5 * up * (1.0 + lax.erf(up * F32(0.7071067811865476)))).astype(BF)
            piece = dot(inner, down_s[n, cols, :])
            total = piece if total is None else total + piece
    part_ref[...] = total.astype(BF)


def middle(weights, attended, hidden, out_bias, gain, shift, bias_own, bias_mate):
    half = ROWS // 2
    return pl.pallas_call(
        middle_kernel,
        out_shape=(
            jax.ShapeDtypeStruct((half, 1024), BF),
            jax.ShapeDtypeStruct((half, 1024), BF),
        ),
        in_specs=[anywhere()] * 12 + [whole()] * 6,
        out_specs=(whole(), whole()),
        scratch_shapes=[
            pltpu.VMEM((2, 1024, 1024), BF),
            pltpu.VMEM((2, 1024, 1024), BF),
            pltpu.VMEM((4, 256, 1024), BF),
            pltpu.VMEM((4, half, 256), BF),
            pltpu.SemaphoreType.DMA((12,)),
        ],
        compiler_params=params(),
        name="middle",
    )(*weights, *attended, hidden, out_bias, gain, shift, bias_own, bias_mate)


def final_kernel(own, other, normed, bias, gain, shift, out_ref):
    lowered = own[...].astype(F32) + other[...].astype(F32)
    total = lowered + bias[...] + normed[...].astype(F32)
    out_ref[...] = normalize(total, gain[1:2, :], shift[1:2, :]).astype(BF)


def final(own, other, normed, bias, gain, shift):
    return pl.pallas_call(
        final_kernel,
        out_shape=jax.ShapeDtypeStruct(own.shape, BF),
        in_specs=[whole()] * 6,
        out_specs=whole(),
        compiler_params=params(),
        name="final",
    )(own, other, normed, bias, gain, shift)


def from_ring(value, by):
    pairs = [
        (z * 8 + ((x + by) % DEPTH) * 2 + y, z * 8 + x * 2 + y)
        for z in range(4)
        for x in range(DEPTH)
        for y in range(2)
    ]
    return lax.ppermute(value, "seq", pairs)


def from_tp(value, flip):
    return lax.ppermute(value, "tp", [(i, i ^ flip) for i in range(4)])


def shards(
    hidden_in, query_weight, query_bias, keyval_weight, keyval_bias, out_weight, out_bias,
    up_weight, up_bias, down_weight, down_bias, norm_gain, norm_bias, prefix_keys,
    prefix_values, suffix_lengths, request_group, owner_group,
):
    core = lax.axis_index("tp") % 2
    prefix = jnp.stack((prefix_keys, prefix_values))
    kv_up, kv_down = from_ring(prefix, 1), from_ring(prefix, 3)
    k_far = from_ring(kv_up[0], 1)
    out_across, out_corner = from_tp(out_weight, 2), from_tp(out_weight, 3)
    q_copies, own_suffix = project(hidden_in, query_weight, query_bias, keyval_weight, keyval_bias)
    cols = prefix_values.shape[1]
    bundle = jnp.concatenate((kv_down[1], own_suffix.reshape(2 * ROWS, cols)), axis=0)
    far_bundle = from_ring(bundle, 3)
    back_two = from_ring(own_suffix, 2)
    queries = lax.all_to_all(q_copies, "seq", 0, 0, tiled=True, axis_index_groups=SEQ_PLANES)
    scalars = (suffix_lengths, request_group, owner_group)
    acc, total, shift, fast = attend(
        True,
        (0, 1, 3),
        scalars,
        (),
        queries,
        (prefix_keys, prefix_values, kv_up, kv_down),
        (),
    )
    acc, k_far, far_bundle, back_two, out_across, out_corner, *late = lax.optimization_barrier(
        (acc, k_far, far_bundle, back_two, out_across, out_corner)
        + (up_weight, down_weight, out_weight, up_bias)
    )
    up_late, down_late, out_late, bias_late = late
    up_mate, down_mate, out_mate = (from_tp(w, 1) for w in (up_late, down_late, out_late))
    bias_mate = from_tp(bias_late.reshape(1, -1), 1)
    parts = attend(
        False,
        (2,),
        scalars,
        (fast,),
        queries,
        (k_far, far_bundle),
        (own_suffix, back_two, acc, total, shift),
    )
    parts, up_mate, down_mate, out_mate, bias_mate = lax.optimization_barrier(
        (parts, up_mate, down_mate, out_mate, bias_mate)
    )
    parts = lax.all_to_all(parts, "seq", 0, 0, tiled=True, axis_index_groups=SEQ_PLANES)
    keep, give = merge(parts)
    normed, part = middle(
        (up_weight, up_mate, down_weight, down_mate, out_weight, out_mate, out_across, out_corner),
        (keep, from_tp(give, 1), from_tp(keep, 2), from_tp(give, 3)),
        hidden_in,
        out_bias.reshape(1, -1),
        norm_gain,
        norm_bias,
        up_bias.reshape(1, -1),
        bias_mate,
    )
    result = final(part, from_tp(part, 2), normed, down_bias.reshape(1, -1), norm_gain, norm_bias)
    other = from_tp(result, 1)
    own_half = lax.broadcasted_iota(jnp.int32, (2, 1, 1), 0) == core
    return jnp.where(own_half, result[None], other[None]).reshape(ROWS, result.shape[1])


def solution(mesh):
    return jax.shard_map(
        shards,
        mesh=mesh,
        in_specs=(
            P("seq", None),
            P(None, "tp"),
            P("tp"),
            P(None, None, "tp"),
            P(None, "tp"),
            P("tp", None),
            P(),
            P(None, "tp"),
            P("tp"),
            P("tp", None),
            P(),
            P(),
            P(),
            P("seq", "tp"),
            P("seq", "tp"),
            P(),
            P(),
            P(),
        ),
        out_specs=P("seq", None),
        check_vma=False,
    )
```

```python
import functools

import jax
import jax.numpy as jnp
from jax import lax
from jax.experimental import pallas as pl
from jax.experimental.pallas import tpu as pltpu
from jax.sharding import PartitionSpec as P

BF = jnp.bfloat16
F32 = jnp.float32
NEG = -1e30
HD = 64
ROWS = 256
PLANE = 8
DEPTH = 4
SUFFIX = 3
TILE = 128
PFX = 1024
TOKENS = 8192
REQS = 48
STATS = 16
VMEM_BYTES = 60 * 1024 * 1024

SEQ_PLANES = [[z * 8 + x * 2 + y for z in range(4) for y in range(2)] for x in range(DEPTH)]


def params(semantics=None):
    return pltpu.CompilerParams(vmem_limit_bytes=VMEM_BYTES, dimension_semantics=semantics)


def whole():
    return pl.BlockSpec(memory_space=pltpu.VMEM)


def anywhere():
    return pl.BlockSpec(memory_space=pl.ANY)


def smem():
    return pl.BlockSpec(memory_space=pltpu.SMEM)


def nt_dot(left, right):
    return lax.dot_general(left, right, (((1,), (1,)), ((), ())), preferred_element_type=F32)


def dot(left, right):
    return jnp.dot(left, right, preferred_element_type=F32)


def project_kernel(x_ref, wq_ref, bq_ref, wkv_ref, bkv_ref, q_ref, kv_ref):
    x = x_ref[...]
    q = (dot(x, wq_ref[...]) + bq_ref[...]).astype(BF) * BF(0.125)
    for n in range(PLANE):
        q_ref[n] = q
    for n in range(2):
        kv_ref[n] = (dot(x, wkv_ref[n]) + bkv_ref[n : n + 1, :]).astype(BF)


def project(x, wq, bq, wkv, bkv):
    cols = wq.shape[1]
    return pl.pallas_call(
        project_kernel,
        out_shape=(
            jax.ShapeDtypeStruct((PLANE, ROWS, cols), BF),
            jax.ShapeDtypeStruct((2, ROWS, cols), BF),
        ),
        in_specs=[whole()] * 5,
        out_specs=(whole(), whole()),
        compiler_params=params(),
        name="project",
    )(x, wq, bq.reshape(1, cols), wkv, bkv)


BOUND = 70.0
WIDE = PLANE * ROWS
TILES = WIDE // TILE


def squares(rows, spread):
    wide = rows.astype(F32)
    return dot((wide * wide).astype(BF), spread)


def attend_kernel(first, shifts, *refs):
    shards = len(shifts)
    lengths, groups, owners = refs[:3]
    refs = refs[3:]
    if first:
        q_hbm, own_k, own_v, kv_up, kv_down = refs[:5]
        kv_hbm = (own_k, own_v, kv_up.at[0], kv_up.at[1], kv_down.at[0], kv_down.at[1])
        refs = refs[5:]
        acc_out, total_out, ref_out, fast_ref = refs[:4]
        refs = refs[4:]
    else:
        fast_in = refs[0]
        q_hbm = refs[1]
        far_k, far_bundle, own_suffix, back_two = refs[2:6]
        acc_in, total_in, ref_in, out_ref = refs[6:10]
        refs = refs[10:]
        kv_hbm = (far_k, far_bundle.at[0:PFX])
        suffixes = (
            (own_suffix.at[0], own_suffix.at[1]),
            (far_bundle.at[PFX : PFX + ROWS], far_bundle.at[PFX + ROWS : PFX + 2 * ROWS]),
            (back_two.at[0], back_two.at[1]),
        )
    acc, total, shift_s, q_s, k_s, v_s, ks_s, vs_s, starts, sem = refs

    place = lax.axis_index("seq")
    ring = (place // 2) % DEPTH
    line = place - 2 * ring

    early = [pltpu.make_async_copy(q_hbm, q_s, sem.at[0])]
    late = []
    for n in range(shards):
        early.append(pltpu.make_async_copy(kv_hbm[2 * n], k_s.at[n], sem.at[1 + 2 * n]))
        late.append(pltpu.make_async_copy(kv_hbm[2 * n + 1], v_s.at[n], sem.at[2 + 2 * n]))
    n_sem = 1 + 2 * shards
    if not first:
        for n in range(SUFFIX):
            early.append(pltpu.make_async_copy(suffixes[n][0], ks_s.at[n], sem.at[n_sem]))
            late.append(pltpu.make_async_copy(suffixes[n][1], vs_s.at[n], sem.at[n_sem + 1]))
            n_sem += 2
        late.append(pltpu.make_async_copy(acc_in, acc, sem.at[n_sem]))
        late.append(pltpu.make_async_copy(total_in, total, sem.at[n_sem + 1]))
        n_sem += 2
    for c in early + late:
        c.start()

    def add_start(r, done):
        starts[r] = done
        return done + lengths[r]

    starts[REQS] = lax.fori_loop(0, REQS, add_start, jnp.int32(0))

    lane = lax.broadcasted_iota(jnp.int32, (TILE, 128), 1)
    low = lane < HD
    wide_head = lax.broadcasted_iota(jnp.int32, (TILE, 256), 1) // HD
    row_head = lax.broadcasted_iota(jnp.int32, (256, 128), 0) // HD
    spread = (row_head == lax.broadcasted_iota(jnp.int32, (256, 128), 1)).astype(F32).astype(BF)
    for c in early:
        c.wait()

    if not first:
        moved = pltpu.make_async_copy(ref_in, shift_s, sem.at[n_sem])
        slow_before = 1 - fast_in[0]

        @pl.when(slow_before > 0)
        def _():
            moved.start()
            moved.wait()

        @pl.when(slow_before == 0)
        def _():
            shift_s[...] = jnp.zeros((WIDE, 256), F32)

    key_top = jnp.max(squares(k_s[0], spread), axis=0, keepdims=True)
    for n in range(1, shards):
        key_top = jnp.maximum(key_top, jnp.max(squares(k_s[n], spread), axis=0, keepdims=True))
    if not first:
        for n in range(SUFFIX):
            top = jnp.max(squares(ks_s[n], spread), axis=0, keepdims=True)
            key_top = jnp.maximum(key_top, top)

    query_top = jnp.max(squares(q_s[...], spread), axis=0, keepdims=True)
    fast = (jnp.max(query_top * key_top) < BOUND * BOUND / 1.05).astype(jnp.int32)
    if not first:
        fast = fast * fast_in[0]
    for c in late:
        c.wait()

    owner_of = [owners[line + 2 * ((ring + s) % DEPTH)] for s in shifts]

    def stacked(row, s):
        cols = slice(128 * s, 128 * s + 128)
        q = q_s[pl.ds(row, TILE), cols]
        zero = jnp.zeros_like(q)
        return jnp.concatenate([jnp.where(low, q, zero), jnp.where(low, zero, q)], axis=0)

    def by_head(pair):
        return jnp.where(low, pair[:TILE], pair[TILE:])

    def four(stack):
        rows = [stack[TILE * h : TILE * h + TILE] for h in range(4)]
        upper = jnp.where(wide_head == 2, rows[2], rows[3])
        return jnp.where(wide_head == 0, rows[0], jnp.where(wide_head == 1, rows[1], upper))

    def step_fast(row, keys, values, ok, mask):
        q = q_s[pl.ds(row, TILE), :]
        zero = jnp.zeros_like(q)
        stack = jnp.concatenate([jnp.where(wide_head == h, q, zero) for h in range(4)], axis=0)
        weights = jnp.exp(nt_dot(stack, keys[...]))
        if mask is not None:
            weights = jnp.where(jnp.concatenate([mask] * 4, axis=0), weights, 0.0)
        sums = weights[:, 0:128]
        for n in range(1, keys.shape[0] // 128):
            sums = sums + weights[:, 128 * n : 128 * n + 128]
        sums = jnp.sum(sums, axis=1, keepdims=True)
        part = dot(weights.astype(BF), values[...])
        acc[pl.ds(row, TILE), :] += jnp.where(ok, four(part), 0.0)
        total[pl.ds(row, TILE), :] += jnp.where(ok, four(sums), 0.0)

    def step_slow(row, keys, values, ok, mask):
        for s in range(2):
            cols = slice(128 * s, 128 * s + 128)
            scores = nt_dot(stacked(row, s), keys[:, cols])
            if mask is not None:
                mask2 = jnp.concatenate([mask, mask], axis=0)
                scores = jnp.where(mask2, scores, NEG)
            top = jnp.max(scores, axis=1, keepdims=True)
            before = total[pl.ds(row, TILE), cols]
            old = jnp.where(before > 0.0, shift_s[pl.ds(row, TILE), cols], NEG)
            tops = by_head(jnp.broadcast_to(top, (2 * TILE, 128)))
            new = jnp.where(ok, jnp.maximum(old, tops), old)
            used = jnp.concatenate([new[:, 0:1], new[:, 64:65]], axis=0)
            ok2 = jnp.concatenate([ok, ok], axis=0)
            weights = jnp.exp(scores - jnp.where(ok2, used, top))
            if mask is not None:
                weights = jnp.where(mask2, weights, 0.0)
            part = dot(weights.astype(BF), values[:, cols])
            sums = jnp.sum(weights, axis=1, keepdims=True)
            sums = jnp.broadcast_to(sums, (2 * TILE, 128))
            fade = jnp.exp(old - new)
            acc[pl.ds(row, TILE), cols] = acc[pl.ds(row, TILE), cols] * fade + jnp.where(
                ok, by_head(part), 0.0
            )
            total[pl.ds(row, TILE), cols] = before * fade + jnp.where(ok, by_head(sums), 0.0)
            shift_s[pl.ds(row, TILE), cols] = jnp.where(ok, new, shift_s[pl.ds(row, TILE), cols])

    def tile_step(t, request):
        row = pl.multiple_of(t * TILE, TILE)
        member = t * TILE // ROWS
        block = (member // 2) * 8 + ring * 2 + member % 2
        token0 = block * ROWS + (t * TILE) % ROWS
        if first:
            acc[pl.ds(row, TILE), :] = jnp.zeros((TILE, 256), F32)
            total[pl.ds(row, TILE), :] = jnp.zeros((TILE, 256), F32)

            @pl.when(fast == 0)
            def _():
                shift_s[pl.ds(row, TILE), :] = jnp.zeros((TILE, 256), F32)

        request = lax.while_loop(lambda r: starts[r + 1] <= token0, lambda r: r + 1, request)
        token = token0 + lax.broadcasted_iota(jnp.int32, (TILE, 1), 0)

        def more(c):
            r = c[0]
            return (r < REQS) & (starts[jnp.minimum(r, REQS)] < token0 + TILE)

        def visit(c):
            r, bits, group, start = c
            here = token >= starts[r]
            g = groups[r]
            return (
                r + 1,
                bits | (jnp.int32(1) << g),
                jnp.where(here, g, group),
                jnp.where(here, starts[r], start),
            )

        zeros = jnp.zeros((TILE, 1), jnp.int32)
        _, bits, group, start = lax.while_loop(more, visit, (request, jnp.int32(0), zeros, zeros))

        def shard(j, _):
            g = owner_of[0]
            for n in range(1, shards):
                g = jnp.where(j == n, owner_of[n], g)
            here = (bits >> g) & 1

            @pl.when((here == 1) & (fast == 1))
            def _():
                step_fast(row, k_s.at[j], v_s.at[j], group == g, None)

            @pl.when((here == 1) & (fast == 0))
            def _():
                step_slow(row, k_s.at[j], v_s.at[j], group == g, None)

            return 0

        lax.fori_loop(0, shards, shard, 0)
        if not first:

            def suffix(j, _):
                key0 = (line + 2 * ((ring - j + DEPTH) % DEPTH)) * ROWS
                here = (key0 < token0 + TILE) & (starts[request] < key0 + ROWS)

                def args():
                    key = key0 + lax.broadcasted_iota(jnp.int32, (TILE, ROWS), 1)
                    mask = (key >= start) & (key <= token)
                    ok = (start < key0 + ROWS) & (key0 <= token)
                    return row, ks_s.at[j], vs_s.at[j], ok, mask

                @pl.when(here & (fast == 1))
                def _():
                    step_fast(*args())

                @pl.when(here & (fast == 0))
                def _():
                    step_slow(*args())

                return 0

            lax.fori_loop(0, SUFFIX, suffix, 0)
        else:
            for c in leave(t):
                c.start()
        return request

    def leave(t):
        rows = pl.ds(pl.multiple_of(t * TILE, TILE), TILE)
        return (
            pltpu.make_async_copy(acc.at[rows, :], acc_out.at[rows, :], sem.at[0]),
            pltpu.make_async_copy(total.at[rows, :], total_out.at[rows, :], sem.at[1]),
        )

    lax.fori_loop(0, TILES, tile_step, jnp.int32(0))

    if first:
        fast_ref[0] = fast

        @pl.when(fast == 0)
        def _():
            moved = pltpu.make_async_copy(shift_s, ref_out, sem.at[2])
            moved.start()
            moved.wait()

        pltpu.make_async_copy(acc, acc_out, sem.at[0]).wait()
        pltpu.make_async_copy(total, total_out, sem.at[1]).wait()
    else:

        def finish(b, _):
            for u in range(2):
                row = pl.multiple_of(b * ROWS + u * TILE, TILE)
                lses = []
                for s in range(2):
                    cols = slice(128 * s, 128 * s + 128)
                    summed = total[pl.ds(row, TILE), cols]
                    some = summed > 0.0
                    safe = jnp.where(some, summed, 1.0)
                    part = jnp.where(some, acc[pl.ds(row, TILE), cols] / safe, 0.0)
                    out_ref[b, u * TILE : (u + 1) * TILE, cols] = part.astype(BF)
                    lses.append(
                        jnp.where(some, shift_s[pl.ds(row, TILE), cols] + jnp.log(safe), F32(NEG))
                    )
                flat = jnp.transpose(jnp.where(lane % HD < HD // 2, lses[0], lses[1]))
                rows4 = jnp.concatenate([flat[r : r + 1, :] for r in (0, 64, 32, 96)], axis=0)
                high = rows4.astype(BF).astype(F32)
                mid = (rows4 - high).astype(BF).astype(F32)
                rest4 = rows4 - high - mid
                stats = jnp.concatenate([high, mid, rest4, jnp.zeros_like(high)], axis=0)
                out_ref[b, ROWS : ROWS + STATS, u * TILE : (u + 1) * TILE] = stats.astype(BF)
            return 0

        lax.fori_loop(0, PLANE, finish, 0)


def attend(first, shifts, scalars, flags, q, kvs, extra):
    shards = len(shifts)
    blocks = 1 if first else SUFFIX
    state = jax.ShapeDtypeStruct((WIDE, 256), F32)
    scratch = [
        pltpu.VMEM((WIDE, 256), F32),
        pltpu.VMEM((WIDE, 256), F32),
        pltpu.VMEM((WIDE, 256), F32),
        pltpu.VMEM((WIDE, 256), BF),
        pltpu.VMEM((shards, PFX, 256), BF),
        pltpu.VMEM((shards, PFX, 256), BF),
        pltpu.VMEM((blocks, ROWS, 256), BF),
        pltpu.VMEM((blocks, ROWS, 256), BF),
        pltpu.SMEM((REQS + 1,), jnp.int32),
        pltpu.SemaphoreType.DMA((16,)),
    ]
    if first:
        out_shape = (state, state, state, jax.ShapeDtypeStruct((1,), jnp.int32))
        out_specs = (anywhere(), anywhere(), anywhere(), smem())
    else:
        out_shape = jax.ShapeDtypeStruct((PLANE, ROWS + STATS, 256), BF)
        out_specs = whole()
    small = list(scalars) + list(flags)
    operands = [q.reshape(WIDE, 256)] + list(kvs) + list(extra)
    return pl.pallas_call(
        functools.partial(attend_kernel, first, shifts),
        out_shape=out_shape,
        in_specs=[smem()] * len(small) + [anywhere()] * len(operands),
        out_specs=out_specs,
        scratch_shapes=scratch,
        compiler_params=params(),
        cost_estimate=pl.CostEstimate(
            flops=shards * 8_000_000_000, transcendentals=0, bytes_accessed=16_000_000
        ),
        name="attend_first" if first else "attend_rest",
    )(*small, *operands)


def merge_kernel(parts_ref, keep_ref, give_ref, out_ref):
    rows = []
    for i in range(PLANE):
        st = parts_ref[i, ROWS : ROWS + STATS, :].astype(F32)
        rows.append(st[0:4] + st[4:8] + st[8:12])
    top = functools.reduce(jnp.maximum, rows)
    rows = [jnp.exp(r - top) for r in rows]
    total = functools.reduce(jnp.add, rows)
    weights = jnp.concatenate([r / total for r in rows], axis=0)
    weights = jnp.concatenate([weights, jnp.zeros((128 - 4 * PLANE, ROWS), F32)], axis=0)
    tall = jnp.transpose(weights)
    high = tall.astype(BF)
    rest = (tall - high.astype(F32)).astype(BF)
    both = jnp.concatenate([high, rest], axis=1)
    source = lax.broadcasted_iota(jnp.int32, (256, 256), 0) % 128
    column_head = lax.broadcasted_iota(jnp.int32, (256, 256), 1) // HD
    acc = jnp.zeros((ROWS, 256), F32)
    for i in range(PLANE):
        spread = (source == column_head + 4 * i).astype(F32).astype(BF)
        acc = acc + dot(both, spread) * parts_ref[i, 0:ROWS, :].astype(F32)
    out_ref[...] = acc
    half = ROWS // 2
    core = lax.axis_index("tp") % 2
    keep_row = pl.multiple_of(core * half, half)
    give_row = pl.multiple_of((1 - core) * half, half)
    give_ref[...] = out_ref[pl.ds(give_row, half), :].astype(BF)
    keep_ref[...] = out_ref[pl.ds(keep_row, half), :].astype(BF)


def merge(parts):
    half = jax.ShapeDtypeStruct((ROWS // 2, 256), BF)
    return pl.pallas_call(
        merge_kernel,
        out_shape=(half, half),
        in_specs=[whole()],
        out_specs=(whole(), whole()),
        scratch_shapes=[pltpu.VMEM((ROWS, 256), F32)],
        compiler_params=params(),
        name="merge",
    )(parts)


def normalize(values, gain, shift):
    center = values - jnp.mean(values, axis=-1, keepdims=True)
    spread = jnp.mean(center * center, axis=-1, keepdims=True)
    return center * lax.rsqrt(spread + 1e-05) * gain + shift


def middle_kernel(
    up_own, up_mate, down_own, down_mate, ow_0, ow_1, ow_2, ow_3, mine, mate, across, corner, hidden_ref,
    out_bias, gain, shift, bias_own, bias_mate, normed_ref, part_ref,
    up_s, down_s, out_s, a_s, sem,
):
    place = lax.axis_index("tp")
    core = place % 2
    other = 1 - core
    side = place - core
    far = 2 - side
    copies = [
        pltpu.make_async_copy(mine, a_s.at[side + core], sem.at[0]),
        pltpu.make_async_copy(mate, a_s.at[side + other], sem.at[1]),
        pltpu.make_async_copy(across, a_s.at[far + core], sem.at[2]),
        pltpu.make_async_copy(corner, a_s.at[far + other], sem.at[3]),
        pltpu.make_async_copy(ow_0, out_s.at[side + core], sem.at[4]),
        pltpu.make_async_copy(ow_1, out_s.at[side + other], sem.at[9]),
        pltpu.make_async_copy(ow_2, out_s.at[far + core], sem.at[10]),
        pltpu.make_async_copy(ow_3, out_s.at[far + other], sem.at[11]),
        pltpu.make_async_copy(up_own, up_s.at[0], sem.at[5]),
        pltpu.make_async_copy(up_mate, up_s.at[1], sem.at[6]),
        pltpu.make_async_copy(down_own, down_s.at[0], sem.at[7]),
        pltpu.make_async_copy(down_mate, down_s.at[1], sem.at[8]),
    ]
    for c in copies:
        c.start()
    half = ROWS // 2
    row = pl.multiple_of(core * half, half)
    for c in copies[:8]:
        c.wait()
    mixed = out_bias[...] + hidden_ref[pl.ds(row, half), :].astype(F32)
    attended = jnp.concatenate([a_s[n] for n in range(4)], axis=1)
    mixed = mixed + dot(attended, out_s[...].reshape(1024, 1024))
    normed = normalize(mixed, gain[0:1, :], shift[0:1, :]).astype(BF)
    normed_ref[...] = normed
    total = None
    biases = (bias_own, bias_mate)
    for n in range(2):
        copies[8 + n].wait()
        copies[10 + n].wait()
        for c in range(2):
            cols = slice(512 * c, 512 * c + 512)
            up = dot(normed, up_s[n, :, cols]) + biases[n][:, cols]
            inner = (0.5 * up * (1.0 + lax.erf(up * F32(0.7071067811865476)))).astype(BF)
            piece = dot(inner, down_s[n, cols, :])
            total = piece if total is None else total + piece
    part_ref[...] = total.astype(BF)


def middle(weights, attended, hidden, out_bias, gain, shift, bias_own, bias_mate):
    half = ROWS // 2
    return pl.pallas_call(
        middle_kernel,
        out_shape=(
            jax.ShapeDtypeStruct((half, 1024), BF),
            jax.ShapeDtypeStruct((half, 1024), BF),
        ),
        in_specs=[anywhere()] * 12 + [whole()] * 6,
        out_specs=(whole(), whole()),
        scratch_shapes=[
            pltpu.VMEM((2, 1024, 1024), BF),
            pltpu.VMEM((2, 1024, 1024), BF),
            pltpu.VMEM((4, 256, 1024), BF),
            pltpu.VMEM((4, half, 256), BF),
            pltpu.SemaphoreType.DMA((12,)),
        ],
        compiler_params=params(),
        name="middle",
    )(*weights, *attended, hidden, out_bias, gain, shift, bias_own, bias_mate)


def final_kernel(own, other, normed, bias, gain, shift, out_ref):
    lowered = own[...].astype(F32) + other[...].astype(F32)
    total = lowered + bias[...] + normed[...].astype(F32)
    out_ref[...] = normalize(total, gain[1:2, :], shift[1:2, :]).astype(BF)


def final(own, other, normed, bias, gain, shift):
    return pl.pallas_call(
        final_kernel,
        out_shape=jax.ShapeDtypeStruct(own.shape, BF),
        in_specs=[whole()] * 6,
        out_specs=whole(),
        compiler_params=params(),
        name="final",
    )(own, other, normed, bias, gain, shift)


def from_ring(value, by):
    pairs = [
        (z * 8 + ((x + by) % DEPTH) * 2 + y, z * 8 + x * 2 + y)
        for z in range(4)
        for x in range(DEPTH)
        for y in range(2)
    ]
    return lax.ppermute(value, "seq", pairs)


def from_tp(value, flip):
    return lax.ppermute(value, "tp", [(i, i ^ flip) for i in range(4)])


def shards(
    hidden_in, query_weight, query_bias, keyval_weight, keyval_bias, out_weight, out_bias,
    up_weight, up_bias, down_weight, down_bias, norm_gain, norm_bias, prefix_keys,
    prefix_values, suffix_lengths, request_group, owner_group,
):
    core = lax.axis_index("tp") % 2
    prefix = jnp.stack((prefix_keys, prefix_values))
    kv_up, kv_down = from_ring(prefix, 1), from_ring(prefix, 3)
    k_far = from_ring(kv_up[0], 1)
    out_across, out_corner = from_tp(out_weight, 2), from_tp(out_weight, 3)
    q_copies, own_suffix = project(hidden_in, query_weight, query_bias, keyval_weight, keyval_bias)
    cols = prefix_values.shape[1]
    bundle = jnp.concatenate((kv_down[1], own_suffix.reshape(2 * ROWS, cols)), axis=0)
    far_bundle = from_ring(bundle, 3)
    back_two = from_ring(own_suffix, 2)
    queries = lax.all_to_all(q_copies, "seq", 0, 0, tiled=True, axis_index_groups=SEQ_PLANES)
    scalars = (suffix_lengths, request_group, owner_group)
    acc, total, shift, fast = attend(
        True,
        (0, 1, 3),
        scalars,
        (),
        queries,
        (prefix_keys, prefix_values, kv_up, kv_down),
        (),
    )
    acc, k_far, far_bundle, back_two, out_across, out_corner, *late = lax.optimization_barrier(
        (acc, k_far, far_bundle, back_two, out_across, out_corner)
        + (up_weight, down_weight, out_weight, up_bias)
    )
    up_late, down_late, out_late, bias_late = late
    up_mate, down_mate, out_mate = (from_tp(w, 1) for w in (up_late, down_late, out_late))
    bias_mate = from_tp(bias_late.reshape(1, -1), 1)
    parts = attend(
        False,
        (2,),
        scalars,
        (fast,),
        queries,
        (k_far, far_bundle),
        (own_suffix, back_two, acc, total, shift),
    )
    parts, up_mate, down_mate, out_mate, bias_mate = lax.optimization_barrier(
        (parts, up_mate, down_mate, out_mate, bias_mate)
    )
    parts = lax.all_to_all(parts, "seq", 0, 0, tiled=True, axis_index_groups=SEQ_PLANES)
    keep, give = merge(parts)
    normed, part = middle(
        (up_weight, up_mate, down_weight, down_mate, out_weight, out_mate, out_across, out_corner),
        (keep, from_tp(give, 1), from_tp(keep, 2), from_tp(give, 3)),
        hidden_in,
        out_bias.reshape(1, -1),
        norm_gain,
        norm_bias,
        up_bias.reshape(1, -1),
        bias_mate,
    )
    result = final(part, from_tp(part, 2), normed, down_bias.reshape(1, -1), norm_gain, norm_bias)
    other = from_tp(result, 1)
    own_half = lax.broadcasted_iota(jnp.int32, (2, 1, 1), 0) == core
    return jnp.where(own_half, result[None], other[None]).reshape(ROWS, result.shape[1])


def solution(mesh):
    return jax.shard_map(
        shards,
        mesh=mesh,
        in_specs=(
            P("seq", None),
            P(None, "tp"),
            P("tp"),
            P(None, None, "tp"),
            P(None, "tp"),
            P("tp", None),
            P(),
            P(None, "tp"),
            P("tp"),
            P("tp", None),
            P(),
            P(),
            P(),
            P("seq", "tp"),
            P("seq", "tp"),
            P(),
            P(),
            P(),
        ),
        out_specs=P("seq", None),
        check_vma=False,
    )
```
